32 devices in a mesh: tm: 2 (over x), lat: 16 (over z, y, core).
Axes of the slice: x: 2, y: 2, z: 4, core: 2. Of those that a mesh axis runs over, the one named last changes fastest.
Arguments:
- starts: float32 [2, 3, 8, 256, 512], P('tm', None, None, 'lat'), may hold values from -1.2 to 1.2
- coarse_old: float32 [2, 3, 8, 128, 256], P('tm', None, None, 'lat'), may hold values from -1.2 to 1.2
- mean_depth: float32 [8], replicated, may hold values from 0.5 to 2
- coupling: float32 [8, 8], replicated, may hold values from 0 to 1, as said below
- wet_cells: int32 [256, 512], P('lat'), may hold values 0 or 1
Outputs:
- new_ends: float32 [2, 3, 8, 256, 512], P('tm', None, None, 'lat')
- coarse_new: float32 [2, 3, 8, 128, 256], P('tm', None, None, 'lat')
The draws below stay inside these ranges and needn't reach their ends.
Inputs may be any that keep to these rules, and one draw needn't show every extreme that they name: `coupling`: symmetric; each diagonal entry is at least 0.6 and exceeds the sum of magnitudes of the other entries of its row.
All inputs are finite; a program needn't handle non-finite values. No bound on the sum of `wet_cells` on one device may be relied on, other than what follows from the above.
Results may differ from the reference program's by a relative error of at most 0.00012.
Values sent between devices are 32-bit elements; how exact they have to be, the bound alone decides.
No kernel may reach another device: no remote copies, remote signals or barrier semaphores. Data moves between devices by JAX's collectives and lax.ppermute only.
A program may use at most 128 MiB of HBM per device.

```python
import math
import jax
import jax.numpy as jnp
from jax import lax

LAYERS = 8
STEPS = 4
NX = 512
NY = 256
SEGMENTS = 2


def draw_coupling(key, part):
    first_key, second_key = jax.random.split(jax.random.fold_in(key, 11))
    spread = 0.5 / (LAYERS - 1)
    offside = jax.random.uniform(first_key, (LAYERS, LAYERS), jnp.float32, 0.3 * spread, spread)
    offside = 0.5 * (offside + offside.T)
    diagonal = jax.random.uniform(second_key, (LAYERS,), jnp.float32, 0.6, 1.0)
    identity = jnp.eye(LAYERS, dtype=jnp.float32)
    return offside * (1.0 - identity) + diagonal[None, :] * identity


def with_ends(values, stream_key, least, high):
    spot = [jax.random.randint(jax.random.fold_in(stream_key, axis), (), 0, length) for axis, length in enumerate(values.shape)]
    widest = values.shape.index(max(values.shape))
    beside = spot[:widest] + [(spot[widest] + 1) % values.shape[widest]] + spot[widest + 1:]
    return values.at[tuple(spot)].set(least).at[tuple(beside)].set(high)


def block_scale(stream_key, shape, cuts, least, largest):
    gain, own = 1.0, jax.random.fold_in(stream_key, 6)
    for dim, blocks in cuts:
        steps = jnp.exp(jax.random.uniform(jax.random.fold_in(own, dim), (blocks,), jnp.float32, least / len(cuts), largest / len(cuts)))
        gain = gain * jnp.repeat(steps, shape[dim] // blocks).reshape([-1 if axis == dim else 1 for axis in range(len(shape))])
    return gain


def scatter_about(rng, dims, width, limit, shards=(), kind=jnp.bfloat16):
    factor_of = block_scale(rng, dims, shards, -0.22, 0.18) if shards else 1.0
    drawn = jax.random.normal(rng, dims, jnp.float32) * width * factor_of
    return jnp.minimum(jnp.maximum(drawn, -limit), limit).astype(kind)


def setup_inputs(seed: int = 0) -> dict:
    keys = jax.random.split(jax.random.key(seed), 6)
    starts = scatter_about(keys[0], (SEGMENTS, 3, LAYERS, NY, NX), 0.3, 1.2, ((0, 2), (3, 16)), jnp.float32)
    coarse_old = scatter_about(keys[1], (SEGMENTS, 3, LAYERS, NY // 2, NX // 2), 0.3, 1.2, ((0, 2), (3, 16)), jnp.float32)
    mean_depth = jnp.clip(jnp.exp(jax.random.uniform(keys[2], (LAYERS,), jnp.float32, math.log(0.5), math.log(2.0))), 0.5, 2.0)
    coupling = draw_coupling(jax.random.fold_in(keys[5], 71), 0)
    wet_cells = with_ends((jax.random.randint(keys[4], (NY, NX), 0, 8) < 7).astype(jnp.int32), jax.random.fold_in(keys[4], 1), 0, 1)
    return {"starts": starts, "coarse_old": coarse_old, "mean_depth": mean_depth, "coupling": coupling, "wet_cells": wet_cells}


time_step = 0.15
viscosity = 0.02
rotation = 0.3


def pad_grid(field):
    field = jnp.concatenate([field[..., -1:], field, field[..., :1]], axis=-1)
    edge_rows = jnp.zeros_like(field[..., :1, :])
    return jnp.concatenate([edge_rows, field, edge_rows], axis=-2)


def gradient_east(values, spacing):
    return (values[..., 1:-1, 2:] - values[..., 1:-1, :-2]) / (2.0 * spacing)


def gradient_north(values, spacing):
    return (values[..., 2:, 1:-1] - values[..., :-2, 1:-1]) / (2.0 * spacing)


def laplacian(values, spacing):
    centre = values[..., 1:-1, 1:-1]
    beside_all = values[..., 2:, 1:-1] + values[..., :-2, 1:-1] + values[..., 1:-1, 2:] + values[..., 1:-1, :-2]
    return (beside_all - 4.0 * centre) / (spacing * spacing)


def coriolis(first_row, count, total):
    rows_here = jnp.arange(count, dtype=jnp.float32) + first_row + 0.5
    return (rotation * (2.0 * rows_here / total - 1.0))[:, None]


def tendency(padded, rotation_rows, wet_mask, mean_depth, coupling, spacing):
    height = padded[..., 0, :, :, :]
    zonal_flow = padded[..., 1, :, :, :]
    merid_flow = padded[..., 2, :, :, :]
    pressure = jnp.einsum("kj,...jrc->...krc", coupling, height, precision=lax.Precision.HIGHEST)
    thickness = mean_depth[:, None, None] + height
    zonal_mid = zonal_flow[..., 1:-1, 1:-1]
    merid_mid = merid_flow[..., 1:-1, 1:-1]
    height_rate = -(gradient_east(thickness * zonal_flow, spacing) + gradient_north(thickness * merid_flow, spacing))
    zonal_rate = -(zonal_mid * gradient_east(zonal_flow, spacing) + merid_mid * gradient_north(zonal_flow, spacing))
    zonal_rate = zonal_rate + rotation_rows * merid_mid - gradient_east(pressure, spacing) + viscosity * laplacian(zonal_flow, spacing)
    merid_rate = -(zonal_mid * gradient_east(merid_flow, spacing) + merid_mid * gradient_north(merid_flow, spacing))
    merid_rate = merid_rate - rotation_rows * zonal_mid - gradient_north(pressure, spacing) + viscosity * laplacian(merid_flow, spacing)
    return jnp.stack([height_rate, wet_mask * zonal_rate, wet_mask * merid_rate], axis=-4)


def fine_run(state, padder, rotation_rows, wet_mask, mean_depth, coupling):
    for repeat in range(STEPS):
        section_one = state + time_step * tendency(padder(state), rotation_rows, wet_mask, mean_depth, coupling, 1.0)
        section_two = 0.75 * state + 0.25 * (section_one + time_step * tendency(padder(section_one), rotation_rows, wet_mask, mean_depth, coupling, 1.0))
        state = state / 3.0 + (2.0 / 3.0) * (section_two + time_step * tendency(padder(section_two), rotation_rows, wet_mask, mean_depth, coupling, 1.0))
    return state


def coarse_step(state, padder, rotation_rows, wet_mask, mean_depth, coupling):
    return state + (STEPS * time_step) * tendency(padder(state), rotation_rows, wet_mask, mean_depth, coupling, 2.0)


def restrict(field):
    return 0.25 * (field[..., 0::2, 0::2] + field[..., 1::2, 0::2] + field[..., 0::2, 1::2] + field[..., 1::2, 1::2])


def prolong(field):
    return jnp.repeat(jnp.repeat(field, 2, axis=-2), 2, axis=-1)


def reference(starts, coarse_old, mean_depth, coupling, wet_cells):
    wet_fine = wet_cells.astype(jnp.float32)
    wet_coarse = wet_fine[0::2, 0::2] * wet_fine[1::2, 0::2] * wet_fine[0::2, 1::2] * wet_fine[1::2, 1::2]
    fine_rows = coriolis(0, NY, NY)
    coarse_rows = coriolis(0, NY // 2, NY // 2)

    def one_segment(start_state):
        return fine_run(start_state, pad_grid, fine_rows, wet_fine, mean_depth, coupling)

    fine_end = lax.map(one_segment, starts)
    delta = restrict(fine_end) - coarse_old
    first_state = restrict(starts[0])

    def link(current, correction):
        result = coarse_step(current, pad_grid, coarse_rows, wet_coarse, mean_depth, coupling)
        return correction + result, result

    unused, coarse_new = lax.scan(link, first_state, delta)
    new_ends = fine_end + prolong(coarse_new - coarse_old)
    return new_ends, coarse_new
```

```python
import functools

import jax
import jax.numpy as jnp
from jax import lax
from jax.experimental import pallas as pl
from jax.experimental.pallas import tpu as pltpu
from jax.sharding import PartitionSpec as P

STEPS = 4
HALO = 3 * STEPS

time_step = 0.15
viscosity = 0.02
rotation = 0.3

STAGE_WEIGHTS = (1.0, 0.25, 2.0 / 3.0)
PRESSURE_ROWS = 8
f32, bf16 = jnp.float32, jnp.bfloat16


def split_two(x):
    high = x.astype(bf16)
    return high, (x - high.astype(f32)).astype(bf16)


def split_three(x):
    high = x.astype(bf16)
    rest = x - high.astype(f32)
    middle = rest.astype(bf16)
    return high, middle, (rest - middle.astype(f32)).astype(bf16)


def tiles_of(x):
    fields, layers, rows, width = x.shape
    x = x.reshape(fields, layers, rows // 8, 8, width // 128, 128).transpose(0, 1, 2, 4, 3, 5)
    return x.reshape(fields, layers * rows * width // 128, 128)


def from_tiles(x, layers, rows, width):
    fields = x.shape[0]
    x = x.reshape(fields, layers, rows // 8, width // 128, 8, 128).transpose(0, 1, 2, 4, 3, 5)
    return x.reshape(fields, layers, rows, width)


def tile_slices(rows, width, r):
    blocks = width // 128
    return [pl.ds(((r // 8) * blocks + c) * 8 + r % 8, 8, stride=rows * blocks) for c in range(blocks)]


def load_row(tiles, field, rows, width, r):
    return jnp.concatenate([tiles[field, part, :] for part in tile_slices(rows, width, r)], axis=1)


def store_row(tiles, field, rows, width, r, value):
    for c, part in enumerate(tile_slices(rows, width, r)):
        tiles[field, part, :] = value[:, c * 128 : (c + 1) * 128]


def dot(a, b):
    return lax.dot_general(a, b, (((1,), (0,)), ((), ())), preferred_element_type=f32)


def east_west(x):
    width = x.shape[-1]
    return pltpu.roll(x, width - 1, 1), pltpu.roll(x, 1, 1)


def row_tendency(source, hv, press, r, depth, twice_viscosity, coriolis):
    e, u, v = source[0, r], source[1, r], source[2, r]
    u_north, u_south = source[1, r + 1], source[1, r - 1]
    v_north, v_south = source[2, r + 1], source[2, r - 1]
    hu_east, hu_west = east_west((depth + e) * u)
    divergence = (hu_east - hu_west) + (hv[r + 1] - hv[r - 1])
    u_east, u_west = east_west(u)
    v_east, v_west = east_west(v)
    p_east, p_west = east_west(press[r])
    to_east, to_west = twice_viscosity - u, twice_viscosity + u
    to_north, to_south = twice_viscosity - v, twice_viscosity + v
    centre = 4.0 * twice_viscosity
    zonal = (to_east * u_east + to_west * u_west) + (to_north * u_north + to_south * u_south)
    zonal = (zonal - (p_east - p_west)) + (coriolis * v - centre * u)
    merid = (to_east * v_east + to_west * v_west) + (to_north * v_north + to_south * v_south)
    merid = (merid - (press[r + 1] - press[r - 1])) - (coriolis * u + centre * v)
    return (e, u, v), (divergence, zonal, merid)


def pressure_rows(source, hv, press, start, count, kron_parts, depth):
    e = source[0, pl.ds(start, count)]
    v = source[2, pl.ds(start, count)]
    hv[pl.ds(start, count)] = (depth + e) * v
    layers, width = e.shape[1:]
    high, low = split_two(e.reshape(count * layers, width))
    kron_high, kron_low = kron_parts
    p = dot(kron_high, high) + dot(kron_high, low) + dot(kron_low, high)
    press[pl.ds(start, count)] = p.reshape(count, layers, width)


def pair_matrix(width, value):
    rows = lax.broadcasted_iota(jnp.int32, (width, width // 2), 0)
    columns = lax.broadcasted_iota(jnp.int32, (width, width // 2), 1)
    return jnp.where((rows >> 1) == columns, value, 0.0).astype(bf16)


def spread_matrix(width):
    rows = lax.broadcasted_iota(jnp.int32, (width // 2, width), 0)
    columns = lax.broadcasted_iota(jnp.int32, (width // 2, width), 1)
    return jnp.where((columns >> 1) == rows, 1.0, 0.0).astype(bf16)


def restrict_rows(state, field, first, count, pairs):
    fine = state[field, first : first + 2 * count]
    layers, width = fine.shape[1:]
    fine = fine.reshape(count, 2, layers, width)
    both = (fine[:, 0] + fine[:, 1]).reshape(count * layers, width)
    high, middle, low = split_three(both)
    coarse = dot(high, pairs) + dot(middle, pairs) + dot(low, pairs)
    return coarse.reshape(count, layers, width // 2)


def coarse_update(state, hv, press, wet, rows, depth, kron_parts, first_coriolis, coriolis_step, emit):
    scale = STEPS * time_step / 4.0
    pressure_rows(state, hv, press, 0, rows + 2, kron_parts, depth)
    for i in range(rows):
        coriolis = first_coriolis + coriolis_step * i
        (e, u, v), (de, du, dv) = row_tendency(state, hv, press, i + 1, depth, viscosity, coriolis)
        mask = wet[i] * scale
        emit(i, (e - scale * de, u + mask * du, v + mask * dv))


def pack_kernel(rows, starts, wet_cells, to_next, to_previous):
    wet = wet_cells[...].astype(f32)
    width = wet.shape[-1]
    planes = 3 * HALO
    for field in range(3):
        for i in range(HALO):
            to_next[field * HALO + i] = load_row(starts, field, rows, width, rows - HALO + i)
            to_previous[field * HALO + i] = load_row(starts, field, rows, width, i)
    to_next[planes] = wet[rows - HALO : rows - HALO + 8]
    to_next[planes + 1] = wet[rows - 8 :]
    to_previous[planes] = wet[:8]
    to_previous[planes + 1] = wet[HALO - 8 : HALO]


def main_kernel(
    rows, scalars, starts, before, after, wet_cells, coarse_old, mean_depth, fine_kron, coarse_kron,
    fine_end, delta, outcome, passed, coarse_wet,
    y, a, b, hv, press, wet, first, chv, cpress,
):
    total = rows + 2 * HALO
    width = wet_cells.shape[-1]
    coarse_rows = rows // 2
    planes = 3 * HALO
    first_coriolis, coriolis_step = scalars[0], scalars[1]
    top, bottom = scalars[2], scalars[3]
    depth = jnp.broadcast_to(mean_depth[...], (8, width))
    coarse_depth = jnp.broadcast_to(mean_depth[...], (8, width // 2))

    for field in range(3):
        y[field, 0:HALO] = before[field * HALO : (field + 1) * HALO]
        y[field, HALO + rows :] = after[field * HALO : (field + 1) * HALO]
        for i in range(rows):
            y[field, HALO + i] = load_row(starts, field, rows, width, i)
    own_wet = wet_cells[...].astype(f32)
    full = time_step / 2.0
    for i in range(HALO):
        place = (i // 8, i % 8) if i < 8 else (1, i - HALO + 8)
        wet[i] = jnp.broadcast_to(before[planes + place[0], place[1]][None] * full, (8, width))
        wet[HALO + rows + i] = jnp.broadcast_to(after[planes + place[0], place[1]][None] * full, (8, width))
    for i in range(rows):
        wet[HALO + i] = jnp.broadcast_to(own_wet[i][None] * full, (8, width))

    pairs = pair_matrix(width, 0.25)
    ones = pair_matrix(width, 1.0)
    for field in range(3):
        first[field] = restrict_rows(y, field, HALO - 2, coarse_rows + 2, pairs)
    for i in range(coarse_rows):
        north = wet[HALO + 2 * i]
        south = wet[HALO + 2 * i + 1]
        both = jnp.where((north > 0.5 * full) & (south > 0.5 * full), 1.0, 0.0).astype(bf16)
        coarse_wet[i] = jnp.maximum(dot(both, ones) - 1.0, 0.0)

    def emit(i, values):
        for field in range(3):
            outcome[field, i] = values[field]

    coarse_update(
        first, chv, cpress, coarse_wet, coarse_rows, coarse_depth, split_two(coarse_kron[...]),
        scalars[4], scalars[5], emit,
    )

    kron_parts = split_two(fine_kron[...])

    def stage(source, target, number, weights, which):
        low, high = number, total - number

        def fill(k, unused):
            start = jnp.minimum(low - 1 + k * PRESSURE_ROWS, high + 1 - PRESSURE_ROWS)
            pressure_rows(source, hv, press, start, PRESSURE_ROWS, kron_parts, depth)
            return unused

        lax.fori_loop(0, (high - low + 2 + PRESSURE_ROWS - 1) // PRESSURE_ROWS, fill, 0)

        factor = STAGE_WEIGHTS[which] * time_step / 2.0

        def one(r):
            coriolis = first_coriolis + coriolis_step * r.astype(f32)
            here, rates = row_tendency(source, hv, press, r, depth, 2.0 * viscosity, coriolis)
            mask = wet[r] * STAGE_WEIGHTS[which]
            inside = jnp.where(r < HALO, top, jnp.where(r >= HALO + rows, bottom, 1.0))
            scales = (-factor * inside, mask, mask)
            for field in range(3):
                value = here[field]
                if weights is not None:
                    value = weights[0] * y[field, r] + weights[1] * value
                target[field, r] = value + scales[field] * rates[field]

        def two(k, unused):
            one(low + 2 * k)
            one(low + 2 * k + 1)
            return unused

        lax.fori_loop(0, (high - low) // 2, two, 0)

    def step(k, unused):
        stage(y, a, 3 * k + 1, None, 0)
        stage(a, b, 3 * k + 2, (0.75, 0.25), 1)
        stage(b, y, 3 * k + 3, (1.0 / 3.0, 2.0 / 3.0), 2)
        return unused

    lax.fori_loop(0, STEPS, step, 0)

    for field in range(3):
        coarse = restrict_rows(y, field, HALO, coarse_rows, pairs)
        for i in range(coarse_rows):
            difference = coarse[i] - load_row(coarse_old, field, coarse_rows, width // 2, i)
            delta[field, i] = difference
            passed[field, i] = difference + outcome[field, i]
        fine_end[field] = y[field, HALO : HALO + rows]


def final_kernel(
    rows, scalars, incoming, before, after, previous, coarse_wet, coarse_old, mean_depth, coarse_kron, fine_end,
    new_ends, coarse_new,
    state, chv, cpress, change,
):
    coarse_rows = rows // 2
    width = fine_end.shape[-1]
    coarse_depth = jnp.broadcast_to(mean_depth[...], (8, width // 2))
    for field in range(3):
        state[field, 0] = before[field]
        state[field, coarse_rows + 1] = after[field]
        state[field, 1 : coarse_rows + 1] = incoming[field]
    last = scalars[6] > 0.5

    def emit(i, values):
        for field in range(3):
            value = jnp.where(last, values[field], previous[field, i])
            store_row(coarse_new, field, coarse_rows, width // 2, i, value)
            change[field, i] = value - load_row(coarse_old, field, coarse_rows, width // 2, i)

    coarse_update(
        state, chv, cpress, coarse_wet, coarse_rows, coarse_depth, split_two(coarse_kron[...]),
        scalars[4], scalars[5], emit,
    )
    spread = spread_matrix(width)
    for field in range(3):
        high, low = split_two(change[field].reshape(coarse_rows * 8, width // 2))
        fine = (dot(high, spread) + dot(low, spread)).reshape(coarse_rows, 8, width)
        for i in range(rows):
            store_row(new_ends, field, rows, width, i, fine_end[field, i] + fine[i // 2])


def middle_turn(incoming, before, after, coarse_wet, mean_depth, coupling, first_coriolis, coriolis_step):
    state = jnp.concatenate([before[:, None], incoming, after[:, None]], axis=1)
    e, u, v = state
    rows = incoming.shape[1]
    p = jnp.einsum("kl,rlc->rkc", coupling, e, precision=lax.Precision.HIGHEST)
    h = mean_depth[None, :, None] + e

    def dx(q):
        return (jnp.roll(q, -1, -1) - jnp.roll(q, 1, -1))[1:-1] / 4.0

    def dy(q):
        return (q[2:] - q[:-2]) / 4.0

    def lap(q):
        return (q[2:] + q[:-2] + (jnp.roll(q, -1, -1) + jnp.roll(q, 1, -1) - 4.0 * q)[1:-1]) / 4.0

    um, vm = u[1:-1], v[1:-1]
    f = (first_coriolis + coriolis_step * jnp.arange(rows, dtype=f32))[:, None, None] / 4.0
    de = -(dx(h * u) + dy(h * v))
    du = coarse_wet * (-(um * dx(u) + vm * dy(u)) + f * vm - dx(p) + viscosity * lap(u))
    dv = coarse_wet * (-(um * dx(v) + vm * dy(v)) - f * um - dy(p) + viscosity * lap(v))
    return incoming + STEPS * time_step * jnp.stack([de, du, dv])


def local(starts, coarse_old, mean_depth, coupling, wet_cells):
    layers, rows, width = starts.shape[2:]
    coarse_rows, half = rows // 2, width // 2
    assert layers == 8 and rows >= HALO
    tm, tm_size = lax.axis_index("tm"), lax.axis_size("tm")
    lat, lat_size = lax.axis_index("lat"), lax.axis_size("lat")
    total_rows = rows * lat_size
    starts = tiles_of(starts[0])
    coarse_old = tiles_of(coarse_old[0])
    vmem = pl.BlockSpec(memory_space=pltpu.VMEM)
    smem = pl.BlockSpec(memory_space=pltpu.SMEM)
    planes = 3 * HALO + 2

    to_next, to_previous = pl.pallas_call(
        functools.partial(pack_kernel, rows),
        out_shape=[jax.ShapeDtypeStruct((planes, 8, width), f32)] * 2,
        in_specs=[vmem] * 2,
        out_specs=[vmem] * 2,
    )(starts, wet_cells)
    up = [(i, i + 1) for i in range(lat_size - 1)]
    down = [(j, i) for i, j in up]
    before = lax.ppermute(to_next, "lat", up)
    after = lax.ppermute(to_previous, "lat", down)

    lat_f = lat.astype(f32)
    slope = 4.0 * rotation / total_rows
    coarse_slope = 16.0 * rotation / total_rows
    scalars = jnp.stack([
        slope * (lat_f * rows - HALO + 0.5) - 2.0 * rotation,
        jnp.asarray(slope, f32),
        (lat > 0).astype(f32),
        (lat < lat_size - 1).astype(f32),
        coarse_slope * (lat_f * coarse_rows + 0.5) - 4.0 * rotation,
        jnp.asarray(coarse_slope, f32),
        (tm == tm_size - 1).astype(f32),
    ])
    depth = mean_depth.reshape(layers, 1)


    def kron(count):
        return (jnp.eye(count, dtype=f32)[:, None, :, None] * coupling[None, :, None, :]).reshape(count * 8, count * 8)

    fine_kron, coarse_kron = kron(PRESSURE_ROWS), kron(coarse_rows + 2)
    coarse_shape = jax.ShapeDtypeStruct((3, coarse_rows, 8, half), f32)
    total = rows + 2 * HALO
    fine_end, delta, outcome, passed, coarse_wet = pl.pallas_call(
        functools.partial(main_kernel, rows),
        out_shape=[
            jax.ShapeDtypeStruct((3, rows, 8, width), f32),
            coarse_shape,
            coarse_shape,
            coarse_shape,
            jax.ShapeDtypeStruct((coarse_rows, 8, half), f32),
        ],
        in_specs=[smem] + [vmem] * 8,
        out_specs=[vmem] * 5,
        scratch_shapes=[pltpu.VMEM((3, total, 8, width), f32)] * 3
        + [pltpu.VMEM((total, 8, width), f32)] * 2
        + [pltpu.VMEM((total, 8, width), f32)]
        + [pltpu.VMEM((3, coarse_rows + 2, 8, half), f32)]
        + [pltpu.VMEM((coarse_rows + 2, 8, half), f32)] * 2,
    )(scalars, starts, before, after, wet_cells, coarse_old, depth, fine_kron, coarse_kron)

    both = ("tm", "lat")

    def hand_on(current):
        def moved(values, shift):
            pairs = [
                (t * lat_size + i, (t + 1) * lat_size + i + shift)
                for t in range(tm_size - 1)
                for i in range(lat_size)
                if 0 <= i + shift < lat_size
            ]
            return lax.ppermute(values, both, pairs)

        return moved(current, 0), moved(current[:, -1], 1), moved(current[:, 0], -1)

    previous = outcome
    incoming = hand_on(passed)
    for turn in range(1, tm_size - 1):
        outcome = middle_turn(*incoming, coarse_wet, mean_depth, coupling, scalars[4], scalars[5])
        previous = jnp.where(tm == turn, outcome, previous)
        incoming = hand_on(delta + outcome)

    new_ends, coarse_new = pl.pallas_call(
        functools.partial(final_kernel, rows),
        out_shape=[
            jax.ShapeDtypeStruct(starts.shape, f32),
            jax.ShapeDtypeStruct(coarse_old.shape, f32),
        ],
        in_specs=[smem] + [vmem] * 9,
        out_specs=[vmem] * 2,
        scratch_shapes=[pltpu.VMEM((3, coarse_rows + 2, 8, half), f32)]
        + [pltpu.VMEM((coarse_rows + 2, 8, half), f32)] * 2
        + [pltpu.VMEM((3, coarse_rows, 8, half), f32)],
    )(scalars, *incoming, previous, coarse_wet, coarse_old, depth, coarse_kron, fine_end)
    return (
        from_tiles(new_ends, layers, rows, width)[None],
        from_tiles(coarse_new, layers, coarse_rows, half)[None],
    )


def solution(mesh):
    in_specs = (
        P("tm", None, None, "lat", None),
        P("tm", None, None, "lat", None),
        P(),
        P(),
        P("lat", None),
    )
    out_specs = (P("tm", None, None, "lat", None), P("tm", None, None, "lat", None))
    return jax.shard_map(local, mesh=mesh, in_specs=in_specs, out_specs=out_specs, check_vma=False)
```

```python
import functools

import jax
import jax.numpy as jnp
import numpy as np
from jax import lax
from jax.experimental import pallas as pl
from jax.experimental.pallas import tpu as pltpu
from jax.sharding import PartitionSpec as P

STEPS = 4
HALO = 3 * STEPS
CHUNK = 8
LANES = 128

time_step = 0.15
viscosity = 0.02
rotation = 0.3

STAGE_WEIGHTS = (1.0, 0.25, 2.0 / 3.0)
STAGE_MIX = (None, (0.75, 0.25), (1.0 / 3.0, 2.0 / 3.0))
f32, bf16 = jnp.float32, jnp.bfloat16


def interleave_matrix(width):
    blocks = width // LANES
    place = np.arange(width)
    columns = blocks * (place % LANES) + place // LANES
    return (np.arange(width)[:, None] == columns[None, :]).astype(np.float32)


def prolong_matrix(width):
    half = width // 2
    blocks = half // LANES
    place = np.arange(half)
    columns = blocks * (place % LANES) + place // LANES
    return (columns[:, None] == np.arange(width)[None, :] // 2).astype(np.float32)


def tiles_of(x):
    fields, layers, rows, width = x.shape
    x = x.reshape(fields, layers, rows // 8, 8, width // LANES, LANES).transpose(0, 1, 2, 4, 3, 5)
    return x.reshape(fields, layers * rows * width // LANES, LANES)


def from_tiles(x, layers, rows, width):
    fields = x.shape[0]
    x = x.reshape(fields, layers, rows // 8, width // LANES, 8, LANES).transpose(0, 1, 2, 4, 3, 5)
    return x.reshape(fields, layers, rows, width)


def tile_slices(rows, width, r):
    blocks = width // LANES
    return [pl.ds(((r // 8) * blocks + c) * 8 + r % 8, 8, stride=rows * blocks) for c in range(blocks)]


def load_row(tiles, field, rows, width, r):
    return jnp.concatenate([tiles[field, part, :] for part in tile_slices(rows, width, r)], axis=1)


def store_row(tiles, field, rows, width, r, value):
    for c, part in enumerate(tile_slices(rows, width, r)):
        tiles[field, part, :] = value[:, c * LANES : (c + 1) * LANES]


def blocks_of(x):
    return [x[:, c : c + LANES] for c in range(0, x.shape[1], LANES)]


def east_west(x):
    blocks = blocks_of(x)
    east = jnp.concatenate(blocks[1:] + [pltpu.roll(blocks[0], LANES - 1, 1)], axis=1)
    west = jnp.concatenate([pltpu.roll(blocks[-1], 1, 1)] + blocks[:-1], axis=1)
    return east, west


def restrict_pair(north, south):
    blocks = blocks_of(north + south)
    return 0.25 * jnp.concatenate([a + b for a, b in zip(blocks[0::2], blocks[1::2])], axis=1)


def split(x, parts):
    found = []
    for _ in range(parts - 1):
        found.append(x.astype(bf16))
        x = x - found[-1].astype(f32)
    return found + [x.astype(bf16)]


def dot(a, b):
    return lax.dot_general(a, b, (((1,), (0,)), ((), ())), preferred_element_type=f32)


def select(x, matrix, parts):
    return sum(dot(part, matrix) for part in split(x, parts))


def coupling_parts(tripled):
    high = tripled.astype(bf16).astype(f32)
    lane = lax.broadcasted_iota(jnp.int32, tripled.shape, 1)
    return jnp.where(lane < 2 * tripled.shape[0], high, tripled - high).astype(bf16)


def pressure_rows(source, hv, press, start, count, kron_parts, depth):
    e = source[0, pl.ds(start, count)]
    v = source[2, pl.ds(start, count)]
    hv[pl.ds(start, count)] = (depth + e) * v
    layers, width = e.shape[1:]
    high, low = split(e.reshape(count * layers, width), 2)
    p = dot(kron_parts, jnp.concatenate([high, low, high], axis=0))
    press[pl.ds(start, count)] = p.reshape(count, layers, width)


def row_tendency(source, hv, press, r, depth, twice_viscosity, coriolis):
    e, u, v = source[0, r], source[1, r], source[2, r]
    u_north, u_south = source[1, r + 1], source[1, r - 1]
    v_north, v_south = source[2, r + 1], source[2, r - 1]
    hu_east, hu_west = east_west((depth + e) * u)
    divergence = (hu_east - hu_west) + (hv[r + 1] - hv[r - 1])
    u_east, u_west = east_west(u)
    v_east, v_west = east_west(v)
    p_east, p_west = east_west(press[r])
    to_east, to_west = twice_viscosity - u, twice_viscosity + u
    to_north, to_south = twice_viscosity - v, twice_viscosity + v
    centre = 4.0 * twice_viscosity
    zonal = (to_east * u_east + to_west * u_west) + (to_north * u_north + to_south * u_south)
    zonal = (zonal - (p_east - p_west)) + (coriolis * v - centre * u)
    merid = (to_east * v_east + to_west * v_west) + (to_north * v_north + to_south * v_south)
    merid = (merid - (press[r + 1] - press[r - 1])) - (coriolis * u + centre * v)
    return (e, u, v), (divergence, zonal, merid)


def run_stage(source, target, base, hv, press, wet, low, high, which, kron_parts, depth, coriolis_of, inside_of):
    count = jnp.maximum(high - low, 0)

    def fill(k, unused):
        start = jnp.minimum(low - 1 + k * CHUNK, high + 1 - CHUNK)
        pressure_rows(source, hv, press, start, CHUNK, kron_parts[...], depth)
        return unused

    chunks = jnp.where(count > 0, (count + 2 + CHUNK - 1) // CHUNK, 0)
    lax.fori_loop(0, chunks, fill, 0)
    factor = STAGE_WEIGHTS[which] * time_step / 2.0
    mix = STAGE_MIX[which]

    def one(r):
        here, rates = row_tendency(source, hv, press, r, depth, 2.0 * viscosity, coriolis_of(r))
        mask = wet[r] * factor
        scales = (-factor * inside_of(r), mask, mask)
        for field in range(3):
            value = here[field]
            if mix is not None:
                value = mix[0] * base[field, r] + mix[1] * value
            target[field, r] = value + scales[field] * rates[field]

    def two(k, unused):
        one(low + 2 * k)
        one(low + 2 * k + 1)
        return unused

    lax.fori_loop(0, count // 2, two, 0)


def coarse_update(state, hv, press, wet, rows, depth, kron_parts, first_coriolis, coriolis_step, emit):
    scale = STEPS * time_step / 4.0
    start = 0
    while start < rows + 2:
        pressure_rows(state, hv, press, min(start, rows + 2 - CHUNK), CHUNK, kron_parts, depth)
        start += CHUNK
    for i in range(rows):
        coriolis = first_coriolis + coriolis_step * i
        (e, u, v), (de, du, dv) = row_tendency(state, hv, press, i + 1, depth, viscosity, coriolis)
        mask = wet[i] * scale
        emit(i, (e - scale * de, u + mask * du, v + mask * dv))


class Fetch:
    def __init__(self, semaphores):
        self.semaphores, self.copies = semaphores, []

    def __call__(self, source, target):
        copy = pltpu.make_async_copy(source, target, self.semaphores.at[len(self.copies)])
        copy.start()
        self.copies.append(copy)

    def wait(self):
        for copy in self.copies:
            copy.wait()


def wet_row(halo, i):
    plane, row = (0, i) if i < 8 else (1, i - HALO + 8)
    return halo[3 * HALO + plane, pl.ds(row, 1), :]


def pack_kernel(rows, starts, wet_cells, matrix, to_next, to_previous):
    width = wet_cells.shape[-1]
    order = matrix[...]
    for field in range(3):
        state = jnp.concatenate([load_row(starts, field, rows, width, i) for i in range(rows)], axis=0)
        state = select(state, order, 2).reshape(rows, 8, width)
        to_next[field * HALO : (field + 1) * HALO] = state[rows - HALO :]
        to_previous[field * HALO : (field + 1) * HALO] = state[:HALO]
    wet = dot(wet_cells[...].astype(f32).astype(bf16), order)
    planes = 3 * HALO
    to_next[planes] = wet[rows - HALO : rows - HALO + 8]
    to_next[planes + 1] = wet[rows - 8 :]
    to_previous[planes] = wet[:8]
    to_previous[planes + 1] = wet[HALO - 8 : HALO]


def inner_kernel(
    rows, scalars, to_next, to_previous, coarse_old, mean_depth, tripled, matrix,
    north_strips, south_strips, coarse_before, first, coarse_wet,
    y, a, b, hv, press, wet, kron_parts,
):
    width = to_next.shape[-1]
    depth = jnp.broadcast_to(mean_depth[...], (8, width))
    kron_parts[...] = coupling_parts(tripled[...])
    for i in range(rows):
        halo, at = (to_previous, i) if i < HALO else (to_next, i - rows + HALO)
        for field in range(3):
            y[field, i] = halo[field * HALO + at]
        wet[i] = jnp.broadcast_to(wet_row(halo, at), (8, width))

    def coriolis_of(r):
        return scalars[0] + scalars[1] * r.astype(f32)

    def keep(state, t):
        for field in range(3):
            north_strips[t, field] = state[field, pl.ds(t, 3)]
            south_strips[t, field] = state[field, pl.ds(rows - 3 - t, 3)]

    keep(y, 0)

    def step(k, unused):
        for which, (source, target) in enumerate(((y, a), (a, b), (b, y))):
            s = 3 * k + which + 1
            run_stage(
                source, target, y, hv, press, wet, s, rows - s, which, kron_parts, depth, coriolis_of, lambda r: 1.0
            )

            @pl.when(s < rows // 2)
            def _():
                keep(target, s)

        return unused

    coarse_rows = rows // 2
    for i in range(coarse_rows):
        both = wet[2 * i] * wet[2 * i + 1]
        blocks = blocks_of(both)
        coarse_wet[i] = jnp.concatenate([p * q for p, q in zip(blocks[0::2], blocks[1::2])], axis=1)
        for field in range(3):
            first[field, i] = restrict_pair(y[field, 2 * i], y[field, 2 * i + 1])
    order = matrix[...]
    for field in range(3):
        old = [load_row(coarse_old, field, coarse_rows, width // 2, i) for i in range(coarse_rows)]
        old = select(jnp.concatenate(old, axis=0), order, 3)
        coarse_before[field] = old.reshape(coarse_rows, 8, width // 2)
    lax.fori_loop(0, (rows // 2 + 1) // 3, step, 0)


def north_kernel(
    rows, scalars, before, to_previous, strips, mean_depth, tripled,
    end_rows, south_strips,
    y, a, b, hv, press, wet, kron_parts, strip, masks, semaphores,
):
    width = y.shape[-1]
    half = rows // 2
    fetch = Fetch(semaphores)
    for field in range(3):
        fetch(before.at[pl.ds(field * HALO, HALO)], y.at[field, pl.ds(0, HALO)])
    fetch(strips, strip)
    fetch(before.at[pl.ds(3 * HALO, 2)], masks.at[0])
    fetch(to_previous.at[pl.ds(3 * HALO, 2)], masks.at[1])
    depth = jnp.broadcast_to(mean_depth[...], (8, width))
    kron_parts[...] = coupling_parts(tripled[...])
    fetch.wait()
    for i in range(HALO + half):
        side, at = (0, i) if i < HALO else (1, i - HALO)
        plane, row = (0, at) if at < 8 else (1, at - HALO + 8)
        wet[i] = jnp.broadcast_to(masks[side, plane, pl.ds(row, 1), :], (8, width))

    def coriolis_of(r):
        return scalars[0] + scalars[1] * (r - HALO).astype(f32)

    def inside_of(r):
        return jnp.where(r < HALO, scalars[2], 1.0)

    def step(k, unused):
        for which, (source, target) in enumerate(((y, a), (a, b), (b, y))):
            t = 3 * k + which
            s = t + 1

            @pl.when(t < half)
            def _():
                for field in range(3):
                    for i in range(3 if which == 0 else 2):
                        source[field, HALO + t + i] = strip[t, field, i]

            high = HALO + jnp.minimum(s, rows - s)
            run_stage(
                source, target, y, hv, press, wet, s, high, which, kron_parts, depth, coriolis_of, inside_of
            )

            @pl.when((s >= half) & (s < HALO))
            def _():
                for field in range(3):
                    south_strips[s - half, field] = target[field, pl.ds(HALO + rows - 3 - s, 3)]

        return unused

    lax.fori_loop(0, STEPS, step, 0)
    for field in range(3):
        end_rows[field] = y[field, HALO : HALO + rows - HALO]


def south_kernel(
    rows, scalars, after, to_next, before, inner_strips, north_strips, first_rows, first, coarse_before, coarse_wet,
    mean_depth, tripled,
    end_rows, delta, outcome, passed,
    y, a, b, hv, press, wet, kron_parts, inner_strip, north_strip, masks, state, edge, old, semaphores,
):
    width = y.shape[-1]
    half = rows // 2
    origin = rows - HALO - 1
    own = rows - origin
    coarse_rows = rows // 2
    fetch = Fetch(semaphores)
    for field in range(3):
        fetch(after.at[pl.ds(field * HALO, HALO)], y.at[field, pl.ds(own, HALO)])
        fetch(before.at[pl.ds(field * HALO + HALO - 2, 2)], edge.at[field])
        fetch(first.at[field], state.at[field, pl.ds(1, coarse_rows)])
    fetch(inner_strips, inner_strip)
    fetch(north_strips, north_strip)
    fetch(after.at[pl.ds(3 * HALO, 2)], masks.at[0])
    fetch(to_next.at[pl.ds(3 * HALO, 2)], masks.at[1])
    fetch(coarse_before, old)
    depth = jnp.broadcast_to(mean_depth[...], (8, width))
    coarse_depth = jnp.broadcast_to(mean_depth[...], (8, width // 2))
    kron_parts[...] = coupling_parts(tripled[...])
    fetch.wait()
    for i in range(HALO):
        plane, row = (0, i) if i < 8 else (1, i - HALO + 8)
        wet[own + i] = jnp.broadcast_to(masks[0, plane, pl.ds(row, 1), :], (8, width))
        wet[own - HALO + i] = jnp.broadcast_to(masks[1, plane, pl.ds(row, 1), :], (8, width))

    for field in range(3):
        state[field, 0] = restrict_pair(edge[field, 0], edge[field, 1])
        state[field, coarse_rows + 1] = restrict_pair(y[field, own], y[field, own + 1])

    def emit(i, values):
        for field in range(3):
            outcome[field, i] = values[field]

    coarse_update(
        state, hv.at[:, :, pl.ds(0, width // 2)], press.at[:, :, pl.ds(0, width // 2)], coarse_wet, coarse_rows,
        coarse_depth, kron_parts[...], scalars[4], scalars[5], emit,
    )

    def coriolis_of(r):
        return scalars[0] + scalars[1] * (r + origin).astype(f32)

    def inside_of(r):
        return jnp.where(r < own, 1.0, scalars[3])

    def step(k, unused):
        for which, (source, target) in enumerate(((y, a), (a, b), (b, y))):
            t = 3 * k + which
            s = t + 1
            skip = 0 if which == 0 else 1

            def insert(strip, index):
                for field in range(3):
                    for i in range(skip, 3):
                        source[field, own - 3 - t + i] = strip[index, field, i]

            @pl.when(t < half)
            def _():
                insert(inner_strip, t)

            @pl.when(t >= half)
            def _():
                insert(north_strip, t - half)

            low = own - s
            run_stage(
                source, target, y, hv, press, wet, low, low + HALO, which, kron_parts, depth, coriolis_of, inside_of
            )
        return unused

    lax.fori_loop(0, STEPS, step, 0)
    early = rows - HALO
    for field in range(3):
        end_rows[field] = y[field, own - HALO : own]
        for i in range(coarse_rows):
            if 2 * i < early:
                pair = first_rows[field, 2 * i], first_rows[field, 2 * i + 1]
            else:
                pair = y[field, 2 * i - origin], y[field, 2 * i + 1 - origin]
            difference = restrict_pair(*pair) - old[field, i]
            delta[field, i] = difference
            passed[field, i] = difference + outcome[field, i]


def natural_kernel(rows, early_rows, late_rows, matrix, natural):
    width = late_rows.shape[-1]
    order = matrix[...]
    for field in range(3):
        for part, first in ((early_rows, 0), (late_rows, rows - HALO)):
            count = part.shape[1]
            value = select(part[field].reshape(count * 8, width), order, 3).reshape(count, 8, width)
            for i in range(count):
                store_row(natural, field, rows, width, first + i, value[i])


def final_kernel(
    rows, scalars, incoming, before, after, previous, coarse_wet, coarse_before, mean_depth, tripled, natural, order,
    spread,
    new_ends, coarse_new,
    state, hv, press, result, semaphores,
):
    coarse_rows = rows // 2
    half = incoming.shape[-1]
    width = 2 * half
    fetch = Fetch(semaphores)
    for field in range(3):
        fetch(before.at[field], state.at[field, 0])
        fetch(after.at[field], state.at[field, coarse_rows + 1])
        fetch(incoming.at[field], state.at[field, pl.ds(1, coarse_rows)])
    coarse_depth = jnp.broadcast_to(mean_depth[...], (8, half))
    kron_parts = coupling_parts(tripled[...])
    last = scalars[6] > 0.5
    fetch.wait()

    def emit(i, values):
        for field in range(3):
            result[field, i] = jnp.where(last, values[field], previous[field, i])

    coarse_update(
        state, hv, press, coarse_wet, coarse_rows, coarse_depth, kron_parts, scalars[4], scalars[5], emit
    )
    to_natural, to_fine = order[...], spread[...]
    for field in range(3):
        value = result[field].reshape(coarse_rows * 8, half)
        change = value - coarse_before[field].reshape(coarse_rows * 8, half)
        fine = select(change, to_fine, 2).reshape(coarse_rows, 8, width)
        value = select(value, to_natural, 2).reshape(coarse_rows, 8, half)
        for i in range(coarse_rows):
            store_row(coarse_new, field, coarse_rows, half, i, value[i])
            for r in (2 * i, 2 * i + 1):
                for c, part in enumerate(tile_slices(rows, width, r)):
                    new_ends[field, part, :] = natural[field, part, :] + fine[i, :, c * LANES : (c + 1) * LANES]


def middle_turn(incoming, before, after, coarse_wet, mean_depth, coupling, first_coriolis, coriolis_step):
    state = jnp.concatenate([before[:, None], incoming, after[:, None]], axis=1)
    e, u, v = state
    rows, layers, half = incoming.shape[1:]
    blocks = half // LANES
    p = jnp.einsum("kl,rlc->rkc", coupling, e, precision=lax.Precision.HIGHEST)
    h = mean_depth[None, :, None] + e

    def dx_parts(q):
        q = q.reshape(q.shape[0], layers, blocks, LANES)
        east = jnp.concatenate([q[:, :, 1:], jnp.roll(q[:, :, :1], -1, -1)], axis=2)
        west = jnp.concatenate([jnp.roll(q[:, :, -1:], 1, -1), q[:, :, :-1]], axis=2)
        return east.reshape(-1, layers, half)[1:-1], west.reshape(-1, layers, half)[1:-1]

    def dx(q):
        east, west = dx_parts(q)
        return (east - west) / 4.0

    def dy(q):
        return (q[2:] - q[:-2]) / 4.0

    def lap(q):
        east, west = dx_parts(q)
        return (q[2:] + q[:-2] + east + west - 4.0 * q[1:-1]) / 4.0

    um, vm = u[1:-1], v[1:-1]
    f = (first_coriolis + coriolis_step * jnp.arange(rows, dtype=f32))[:, None, None] / 4.0
    de = -(dx(h * u) + dy(h * v))
    du = coarse_wet * (-(um * dx(u) + vm * dy(u)) + f * vm - dx(p) + viscosity * lap(u))
    dv = coarse_wet * (-(um * dx(v) + vm * dy(v)) - f * um - dy(p) + viscosity * lap(v))
    return incoming + STEPS * time_step * jnp.stack([de, du, dv])


def local(starts, coarse_old, mean_depth, coupling, wet_cells):
    layers, rows, width = starts.shape[2:]
    coarse_rows, half = rows // 2, width // 2
    assert layers == 8 and rows % 8 == 0 and HALO < rows <= 2 * HALO
    tm, tm_size = lax.axis_index("tm"), lax.axis_size("tm")
    lat, lat_size = lax.axis_index("lat"), lax.axis_size("lat")
    total_rows = rows * lat_size
    starts = tiles_of(starts[0])
    coarse_old = tiles_of(coarse_old[0])
    vmem = pl.BlockSpec(memory_space=pltpu.VMEM)
    smem = pl.BlockSpec(memory_space=pltpu.SMEM)
    anywhere = pl.BlockSpec(memory_space=pl.ANY)
    fine_order = interleave_matrix(width)
    coarse_order = interleave_matrix(half)
    planes = 3 * HALO + 2

    def array(*shape):
        return jax.ShapeDtypeStruct(shape, f32)

    def buffer(*shape):
        return pltpu.VMEM(shape, f32)

    def call(kernel, outs, in_specs, scratch=()):
        return pl.pallas_call(
            functools.partial(kernel, rows),
            out_shape=outs,
            in_specs=in_specs,
            out_specs=[vmem] * len(outs),
            scratch_shapes=list(scratch),
            name=kernel.__name__,
            compiler_params=pltpu.CompilerParams(vmem_limit_bytes=16 * 2**20),
        )

    to_next, to_previous = call(pack_kernel, [array(planes, 8, width)] * 2, [vmem] * 3)(
        starts, wet_cells, jnp.asarray(fine_order, bf16)
    )
    up = [(i, i + 1) for i in range(lat_size - 1)]
    down = [(j, i) for i, j in up]
    before = lax.ppermute(to_next, "lat", up)

    lat_f = lat.astype(f32)
    slope = 4.0 * rotation / total_rows
    coarse_slope = 16.0 * rotation / total_rows
    scalars = jnp.stack([
        slope * (lat_f * rows + 0.5) - 2.0 * rotation,
        jnp.asarray(slope, f32),
        (lat > 0).astype(f32),
        (lat < lat_size - 1).astype(f32),
        coarse_slope * (lat_f * coarse_rows + 0.5) - 4.0 * rotation,
        jnp.asarray(coarse_slope, f32),
        (tm == tm_size - 1).astype(f32),
    ])
    depth = mean_depth.reshape(layers, 1)
    same_row = np.kron(np.eye(CHUNK), np.ones((8, 8))).astype(np.float32)
    tripled = jnp.tile(jnp.tile(coupling, (CHUNK, CHUNK)) * same_row, (1, 3))

    def stage_scratch(count):
        return [buffer(3, count, 8, width)] * 3 + [buffer(count, 8, width)] * 3 + [
            pltpu.VMEM((CHUNK * 8, 3 * CHUNK * 8), bf16)
        ]

    north_strips, south_strips, coarse_before, first, coarse_wet = call(
        inner_kernel,
        [array(rows // 2, 3, 3, 8, width)] * 2
        + [array(3, coarse_rows, 8, half)] * 2
        + [array(coarse_rows, 8, half)],
        [smem] + [vmem] * 6,
        stage_scratch(rows),
    )(scalars, to_next, to_previous, coarse_old, depth, tripled, jnp.asarray(coarse_order, bf16))
    to_previous, south_strips = lax.optimization_barrier((to_previous, south_strips))
    after = lax.ppermute(to_previous, "lat", down)

    early_rows, late_strips = call(
        north_kernel,
        [array(3, rows - HALO, 8, width), array(HALO - rows // 2, 3, 3, 8, width)],
        [smem] + [anywhere] * 3 + [vmem] * 2,
        stage_scratch(HALO + rows)
        + [buffer(rows // 2, 3, 3, 8, width), buffer(2, 2, 8, width), pltpu.SemaphoreType.DMA((6,))],
    )(scalars, before, to_previous, north_strips, depth, tripled)

    late_rows, delta, outcome, passed = call(
        south_kernel,
        [array(3, HALO, 8, width)] + [array(3, coarse_rows, 8, half)] * 3,
        [smem] + [anywhere] * 5 + [vmem] + [anywhere] * 2 + [vmem] * 3,
        stage_scratch(2 * HALO + 1)
        + [buffer(rows // 2, 3, 3, 8, width), buffer(HALO - rows // 2, 3, 3, 8, width), buffer(2, 2, 8, width)]
        + [buffer(3, coarse_rows + 2, 8, half), buffer(3, 2, 8, width), buffer(3, coarse_rows, 8, half)]
        + [pltpu.SemaphoreType.DMA((14,))],
    )(
        scalars, after, to_next, before, south_strips, late_strips, early_rows, first, coarse_before, coarse_wet,
        depth, tripled,
    )

    both = ("tm", "lat")

    def hand_on(current):
        def moved(values, shift):
            pairs = [
                (t * lat_size + i, (t + 1) * lat_size + i + shift)
                for t in range(tm_size - 1)
                for i in range(lat_size)
                if 0 <= i + shift < lat_size
            ]
            return lax.ppermute(values, both, pairs)

        return moved(current, 0), moved(current[:, -1], 1), moved(current[:, 0], -1)

    previous = outcome
    incoming = hand_on(passed)
    (natural,) = call(natural_kernel, [array(*starts.shape)], [vmem] * 3)(
        early_rows, late_rows, jnp.asarray(fine_order.T, bf16)
    )
    for turn in range(1, tm_size - 1):
        outcome = middle_turn(*incoming, coarse_wet, mean_depth, coupling, scalars[4], scalars[5])
        previous = jnp.where(tm == turn, outcome, previous)
        incoming = hand_on(delta + outcome)

    new_ends, coarse_new = call(
        final_kernel,
        [array(*starts.shape), array(*coarse_old.shape)],
        [smem] + [anywhere] * 3 + [vmem] * 8,
        [buffer(3, coarse_rows + 2, 8, half)]
        + [buffer(coarse_rows + 2, 8, half)] * 2
        + [buffer(3, coarse_rows, 8, half), pltpu.SemaphoreType.DMA((9,))],
    )(
        scalars, *incoming, previous, coarse_wet, coarse_before, depth, tripled, natural,
        jnp.asarray(coarse_order.T, bf16), jnp.asarray(prolong_matrix(width), bf16),
    )
    return (
        from_tiles(new_ends, layers, rows, width)[None],
        from_tiles(coarse_new, layers, coarse_rows, half)[None],
    )


def solution(mesh):
    in_specs = (
        P("tm", None, None, "lat", None),
        P("tm", None, None, "lat", None),
        P(),
        P(),
        P("lat", None),
    )
    out_specs = (P("tm", None, None, "lat", None), P("tm", None, None, "lat", None))
    return jax.shard_map(local, mesh=mesh, in_specs=in_specs, out_specs=out_specs, check_vma=False)
```

```python
import functools

import jax
import jax.numpy as jnp
import numpy as np
from jax import lax
from jax.experimental import pallas as pl
from jax.experimental.pallas import tpu as pltpu
from jax.sharding import PartitionSpec as P


STEPS = 4
HALO = 3 * STEPS
GROUP = 6
CHUNK = GROUP + 2
LANES = 128

time_step = 0.15
viscosity = 0.02
rotation = 0.3

STAGE_WEIGHTS = (1.0, 0.25, 2.0 / 3.0)
STAGE_MIX = (None, (0.75, 0.25), (1.0 / 3.0, 2.0 / 3.0))
f32, bf16 = jnp.float32, jnp.bfloat16


def interleave_matrix(width):
    blocks = width // LANES
    place = np.arange(width)
    columns = blocks * (place % LANES) + place // LANES
    return (np.arange(width)[:, None] == columns[None, :]).astype(np.float32)


def prolong_matrix(width):
    half = width // 2
    blocks = half // LANES
    place = np.arange(half)
    columns = blocks * (place % LANES) + place // LANES
    return (columns[:, None] == np.arange(width)[None, :] // 2).astype(np.float32)


def tiles_of(x):
    fields, layers, rows, width = x.shape
    x = x.reshape(fields, layers, rows // 8, 8, width // LANES, LANES).transpose(0, 1, 2, 4, 3, 5)
    return x.reshape(fields, layers * rows * width // LANES, LANES)


def from_tiles(x, layers, rows, width):
    fields = x.shape[0]
    x = x.reshape(fields, layers, rows // 8, width // LANES, 8, LANES).transpose(0, 1, 2, 4, 3, 5)
    return x.reshape(fields, layers, rows, width)


def tile_slices(rows, width, r):
    blocks = width // LANES
    if not isinstance(r, int):
        start = lax.div(r, 8) * (8 * blocks) + lax.rem(r, 8)
    else:
        start = (r // 8) * (8 * blocks) + r % 8
    return [pl.ds(start + 8 * c, 8, stride=rows * blocks) for c in range(blocks)]


def load_row(tiles, field, rows, width, r):
    return jnp.concatenate([tiles[field, part, :] for part in tile_slices(rows, width, r)], axis=1)


def store_row(tiles, field, rows, width, r, value):
    for c, part in enumerate(tile_slices(rows, width, r)):
        tiles[field, part, :] = value[:, c * LANES : (c + 1) * LANES]


def blocks_of(x):
    return [x[:, c : c + LANES] for c in range(0, x.shape[1], LANES)]


def east_west(x):
    blocks = blocks_of(x)
    east = jnp.concatenate(blocks[1:] + [pltpu.roll(blocks[0], LANES - 1, 1)], axis=1)
    west = jnp.concatenate([pltpu.roll(blocks[-1], 1, 1)] + blocks[:-1], axis=1)
    return east, west


def restrict_pair(north, south):
    blocks = blocks_of(north + south)
    return 0.25 * jnp.concatenate([a + b for a, b in zip(blocks[0::2], blocks[1::2])], axis=1)


def split(x, parts):
    found = []
    for _ in range(parts - 1):
        found.append(x.astype(bf16))
        x = x - found[-1].astype(f32)
    return found + [x.astype(bf16)]


def dot(a, b):
    return lax.dot_general(a, b, (((1,), (0,)), ((), ())), preferred_element_type=f32)


def select(x, matrix, parts):
    return sum(dot(part, matrix) for part in split(x, parts))


def coupling_parts(coupling, count):
    size = 8 * count
    high, low = split(jnp.concatenate([coupling] * count, axis=0), 2)
    layer = lax.broadcasted_iota(jnp.int32, (8, 3 * size), 0)
    column = lax.broadcasted_iota(jnp.int32, (8, 3 * size), 1)
    spread = jnp.where((column & 7) == layer, 1.0, 0.0).astype(bf16)
    row = lax.broadcasted_iota(jnp.int32, (size, 3 * size), 0)
    column = lax.broadcasted_iota(jnp.int32, (size, 3 * size), 1)
    third = jnp.where(column >= 2 * size, 2, jnp.where(column >= size, 1, 0))
    parts = jnp.where(third == 2, dot(low, spread), dot(high, spread))
    return jnp.where(((column - size * third) >> 3) == (row >> 3), parts, 0.0).astype(bf16)


def depth_of(mean_depth, width):
    row = lax.broadcasted_iota(jnp.int32, (8, 8), 0)
    column = lax.broadcasted_iota(jnp.int32, (8, 8), 1)
    diagonal = jnp.where(row == column, jnp.broadcast_to(mean_depth[...], (8, 8)), 0.0)
    return select(diagonal, jnp.ones((8, width), bf16), 3)


class Place:
    def __init__(self, rows):
        lat, lat_size = lax.axis_index("lat"), lax.axis_size("lat")
        tm, tm_size = lax.axis_index("tm"), lax.axis_size("tm")
        total = rows * lat_size
        self.even = lax.rem(lat, 2) == 0
        self.last = tm == tm_size - 1
        self.sign = jnp.where(self.even, -1.0, 1.0).astype(f32)
        low, high = (lat > 0).astype(f32), (lat < lat_size - 1).astype(f32)
        self.near_inside = jnp.where(self.even, high, low)
        self.far_inside = jnp.where(self.even, low, high)
        lat_f = lat.astype(f32)
        self.step = 4.0 * rotation / total
        self.coarse_step = 16.0 * rotation / total
        first = self.step * (lat_f * rows + 0.5) - 2.0 * rotation
        coarse = self.coarse_step * (lat_f * (rows // 2) + 0.5) - 4.0 * rotation
        self.first = jnp.where(self.even, -(first + self.step * (rows - 1)), first)
        self.coarse_first = jnp.where(self.even, -(coarse + self.coarse_step * (rows // 2 - 1)), coarse)

    def own_row(self, rows, i):
        return jnp.where(self.even, rows - 1 - i, i)


def pressure_rows(source, hv, press, start, count, kron_parts):
    h = source[0, pl.ds(start, count)]
    hv[pl.ds(start, count)] = h * source[2, pl.ds(start, count)]
    layers, width = h.shape[1:]
    high, low = split(h.reshape(count * layers, width), 2)
    p = dot(kron_parts[count][...], jnp.concatenate([high, low, high], axis=0))
    press[pl.ds(start, count)] = p.reshape(count, layers, width)


def row_tendency(source, hv, press, r, twice_viscosity, coriolis):
    h, u, v = source[0, r], source[1, r], source[2, r]
    u_north, u_south = source[1, r + 1], source[1, r - 1]
    v_north, v_south = source[2, r + 1], source[2, r - 1]
    hu_east, hu_west = east_west(h * u)
    divergence = (hu_east - hu_west) + (hv[r + 1] - hv[r - 1])
    u_east, u_west = east_west(u)
    v_east, v_west = east_west(v)
    p_east, p_west = east_west(press[r])
    to_east, to_west = twice_viscosity - u, twice_viscosity + u
    to_north, to_south = twice_viscosity - v, twice_viscosity + v
    zonal = (to_east * u_east + to_west * u_west) + (to_north * u_north + to_south * u_south)
    zonal = (zonal - (p_east - p_west)) + coriolis * v
    merid = (to_east * v_east + to_west * v_west) + (to_north * v_north + to_south * v_south)
    merid = (merid - (press[r + 1] - press[r - 1])) - coriolis * u
    return (h, u, v), (divergence, zonal, merid)


def run_stage(
    source, target, base, hv, press, wet, low, high, count, which, kron_parts, coriolis_of, inside_of
):
    factor = STAGE_WEIGHTS[which] * time_step / 2.0
    mix = STAGE_MIX[which]

    def one(r):
        here, rates = row_tendency(source, hv, press, r, 2.0 * viscosity, coriolis_of(r))
        mask, keep = wet[which, r], wet[3 + which, r]
        values = [here[0] if mix is None else mix[1] * here[0], keep * here[1], keep * here[2]]
        scales = (-factor * inside_of(r), mask, mask)
        for field in range(3):
            value = values[field]
            if mix is not None:
                value = value + mix[0] * base[field, r]
            target[field, r] = value + scales[field] * rates[field]

    def group(first):
        for i in range(GROUP):
            one(first + i)

    def fill(start, count):
        pressure_rows(source, hv, press, start, count, kron_parts)

    if isinstance(count, int):
        fill(low - 1, GROUP + 2)
        for first in range(0, count, GROUP):
            if first + GROUP < count:
                fill(low + first + GROUP + 1, GROUP)
            group(low + first)
        return

    def turn(k, unused):
        first = low + GROUP * k
        group(first)
        fill(jnp.minimum(first + GROUP + 1, high + 1 - GROUP), GROUP)
        return unused

    def two(k, unused):
        first = high - 2 * (rest - k)
        one(first)
        one(first + 1)
        return unused

    turns = lax.div(count, GROUP)
    rest = lax.div(count - GROUP * turns, 2)
    fill(jnp.minimum(low - 1, high - 1 - GROUP), GROUP + 2)
    lax.fori_loop(0, turns, turn, 0)
    lax.fori_loop(0, rest, two, 0)


def coarse_update(state, hv, press, wet, rows, kron_parts, first_coriolis, coriolis_step, emit):
    scale = STEPS * time_step / 4.0
    start = 0
    while start < rows + 2:
        pressure_rows(state, hv, press, min(start, rows + 2 - CHUNK), CHUNK, kron_parts)
        start += CHUNK
    for i in range(rows):
        coriolis = first_coriolis + coriolis_step * i
        (h, u, v), (dh, du, dv) = row_tendency(state, hv, press, i + 1, viscosity, coriolis)
        mask = wet[i] * scale
        keep = 1.0 - 4.0 * viscosity * mask
        emit(i, (h - scale * dh, keep * u + mask * du, keep * v + mask * dv))


def wet_row(halo, i):
    plane, row = (0, i) if i < 8 else (1, i - HALO + 8)
    return halo[3 * HALO + plane, pl.ds(row, 1), :]


def set_masks(wet, i, mask):
    for which, weight in enumerate(STAGE_WEIGHTS):
        scaled = mask * (weight * time_step / 2.0)
        wet[which, i] = scaled
        wet[3 + which, i] = weight - 8.0 * viscosity * scaled


def turned(x, field):
    return -x if field == 2 else x


def pack_kernel(rows, starts_hbm, wet_hbm, to_near, to_far, starts, wet_cells, wet, semaphores):
    width = wet_cells.shape[-1]
    blocks = width // LANES
    copies = [
        pltpu.make_async_copy(source, target, semaphores.at[n])
        for n, (source, target) in enumerate(
            [(starts_hbm.at[field], starts.at[field]) for field in range(3)] + [(wet_hbm, wet_cells)]
        )
    ]
    for copy in copies:
        copy.start()
    place = Place(rows)
    column = lax.broadcasted_iota(jnp.int32, (width, LANES), 0)
    column = column - blocks * lax.broadcasted_iota(jnp.int32, (width, LANES), 1)
    order = jnp.concatenate([jnp.where(column == c, 1.0, 0.0).astype(bf16) for c in range(blocks)], axis=1)
    for field in range(3):
        copies[field].wait()
        state = [load_row(starts, field, rows, width, place.own_row(rows, i)) for i in range(rows)]
        state = jnp.concatenate(state, axis=0)
        state = select(state * place.sign if field == 2 else state, order, 2).reshape(rows, 8, width)
        to_near[field * HALO : (field + 1) * HALO] = state[:HALO]
        to_far[field * HALO : (field + 1) * HALO] = state[rows - HALO :]
    copies[3].wait()
    wet[...] = dot(wet_cells[...].astype(f32).astype(bf16), order)
    for plane, skip in ((0, 0), (1, HALO - 8)):
        for i in range(8):
            for packed, first in ((to_near, 0), (to_far, rows - HALO)):
                row = place.own_row(rows, first + skip + i)
                packed[3 * HALO + plane, pl.ds(i, 1), :] = wet[pl.ds(row, 1), :]


def near_kernel(
    rows, near, to_near, to_far, coarse_old, mean_depth, coupling, matrix,
    early_rows, strips, coarse_before, first, coarse_wet,
    y, a, b, hv, press, wet, short_parts, long_parts,
):
    width = y.shape[-1]
    coarse_rows = rows // 2
    place = Place(rows)
    depth = depth_of(mean_depth, width)
    kron_parts = {}
    for count, parts in ((GROUP, short_parts), (CHUNK, long_parts)):
        parts[...] = coupling_parts(coupling[...], count)
        kron_parts[count] = parts
    for i in range(HALO):
        for field in range(3):
            value = turned(near[field * HALO + i], field)
            y[field, HALO - 1 - i] = value + depth if field == 0 else value
        set_masks(wet, HALO - 1 - i, jnp.broadcast_to(wet_row(near, i), (8, width)))
    for i in range(rows):
        sent, at = (to_near, i) if i < HALO else (to_far, i - rows + HALO)
        for field in range(3):
            value = sent[field * HALO + at]
            y[field, HALO + i] = value + depth if field == 0 else value
        set_masks(wet, HALO + i, jnp.broadcast_to(wet_row(sent, at), (8, width)))

    def coriolis_of(r):
        return place.first + place.step * (r - HALO).astype(f32)

    def inside_of(r):
        return jnp.where(r < HALO, place.near_inside, 1.0)

    def keep(state, t):
        for field in range(3):
            strips[t, field] = state[field, pl.ds(HALO + rows - 3 - t, 3)]

    keep(y, 0)
    for i in range(coarse_rows):
        both = wet[0, HALO + 2 * i] * wet[0, HALO + 2 * i + 1]
        blocks = blocks_of(jnp.where(both > 0.0, 1.0, 0.0))
        coarse_wet[i] = jnp.concatenate([p * q for p, q in zip(blocks[0::2], blocks[1::2])], axis=1)
        for field in range(3):
            first[field, i] = restrict_pair(y[field, HALO + 2 * i], y[field, HALO + 2 * i + 1])
    order = matrix[...]
    for field in range(3):
        old = [
            load_row(coarse_old, field, coarse_rows, width // 2, place.own_row(coarse_rows, i))
            for i in range(coarse_rows)
        ]
        old = select(jnp.concatenate(old, axis=0), order, 2).reshape(coarse_rows, 8, width // 2)
        if field == 0:
            old = old + depth[:, : width // 2]
        coarse_before[field] = old * place.sign if field == 2 else old

    def step(k, unused):
        for which, (source, target) in enumerate(((y, a), (a, b), (b, y))):
            s = 3 * k + which + 1
            run_stage(
                source, target, y, hv, press, wet, s, HALO + rows - s, HALO + rows - 2 * s, which, kron_parts, coriolis_of, inside_of
            )

            @pl.when(s < HALO)
            def _():
                keep(target, s)

        return unused

    lax.fori_loop(0, STEPS, step, 0)
    for field in range(3):
        early_rows[field] = y[field, HALO : HALO + rows - HALO]


def far_kernel(
    rows, far, to_far, near, strips, early_rows, first, coarse_before, coarse_wet,
    mean_depth, coupling,
    late_rows, delta, outcome, passed,
    y, a, b, hv, press, wet, short_parts, long_parts, state,
):
    width = y.shape[-1]
    origin = rows - HALO - 1
    own = rows - origin
    coarse_rows = rows // 2
    place = Place(rows)
    depth = depth_of(mean_depth, width)
    kron_parts = {}
    for count, parts in ((GROUP, short_parts), (CHUNK, long_parts)):
        parts[...] = coupling_parts(coupling[...], count)
        kron_parts[count] = parts
    for field in range(3):
        for i in range(HALO):
            value = turned(far[(field + 1) * HALO - 1 - i], field)
            y[field, own + i] = value + depth if field == 0 else value
        state[field, 1 : coarse_rows + 1] = first[field]
    for i in range(HALO):
        set_masks(wet, own + i, jnp.broadcast_to(wet_row(far, HALO - 1 - i), (8, width)))
        set_masks(wet, own - HALO + i, jnp.broadcast_to(wet_row(to_far, i), (8, width)))

    for field in range(3):
        edge = turned(restrict_pair(near[field * HALO], near[field * HALO + 1]), field)
        state[field, 0] = edge + depth[:, : width // 2] if field == 0 else edge
        state[field, coarse_rows + 1] = restrict_pair(y[field, own], y[field, own + 1])

    def emit(i, values):
        for field in range(3):
            outcome[field, i] = values[field]

    coarse_update(
        state, hv.at[:, :, pl.ds(0, width // 2)], press.at[:, :, pl.ds(0, width // 2)], coarse_wet, coarse_rows,
        kron_parts, place.coarse_first, place.coarse_step, emit,
    )

    def coriolis_of(r):
        return place.first + place.step * (r + origin).astype(f32)

    def inside_of(r):
        return jnp.where(r < own, 1.0, place.far_inside)

    def step(k, unused):
        for which, (source, target) in enumerate(((y, a), (a, b), (b, y))):
            t = 3 * k + which
            s = t + 1
            for field in range(3):
                for i in range(0 if which == 0 else 1, 3):
                    source[field, own - 3 - t + i] = strips[t, field, i]
            low = own - s
            run_stage(
                source, target, y, hv, press, wet, low, low + HALO, HALO, which, kron_parts, coriolis_of, inside_of
            )
        return unused

    lax.fori_loop(0, STEPS, step, 0)
    early = rows - HALO
    for field in range(3):
        late_rows[field] = y[field, own - HALO : own]
        for i in range(coarse_rows):
            if 2 * i < early:
                pair = early_rows[field, 2 * i], early_rows[field, 2 * i + 1]
            else:
                pair = y[field, 2 * i - origin], y[field, 2 * i + 1 - origin]
            difference = restrict_pair(*pair) - coarse_before[field, i]
            delta[field, i] = difference
            passed[field, i] = difference + outcome[field, i]


def natural_kernel(rows, early_rows, late_rows, mean_depth, matrix, natural):
    width = late_rows.shape[-1]
    order = matrix[...]
    place = Place(rows)
    depth = depth_of(mean_depth, width)
    for field in range(3):
        for part, first in ((early_rows, 0), (late_rows, rows - HALO)):
            count = part.shape[1]
            value = part[field] - depth if field == 0 else part[field]
            if field == 2:
                value = value * place.sign
            value = select(value.reshape(count * 8, width), order, 3).reshape(count, 8, width)
            for i in range(count):
                store_row(natural, field, rows, width, place.own_row(rows, first + i), value[i])


def final_kernel(
    rows, incoming, near_edge, far_edge, previous, coarse_wet, coarse_before, mean_depth, coupling, natural, order,
    spread,
    new_ends, coarse_new,
    state, hv, press, result,
):
    coarse_rows = rows // 2
    half = incoming.shape[-1]
    width = 2 * half
    place = Place(rows)
    depth = depth_of(mean_depth, half)
    for field in range(3):
        state[field, 0] = turned(near_edge[field], field)
        state[field, coarse_rows + 1] = turned(far_edge[field], field)
        state[field, 1 : coarse_rows + 1] = incoming[field]
    state[0, 0] += (1.0 - place.near_inside) * depth
    state[0, coarse_rows + 1] += (1.0 - place.far_inside) * depth
    kron_parts = {CHUNK: coupling_parts(coupling[...], CHUNK)}

    def emit(i, values):
        for field in range(3):
            result[field, i] = jnp.where(place.last, values[field], previous[field, i])

    coarse_update(
        state, hv, press, coarse_wet, coarse_rows, kron_parts, place.coarse_first, place.coarse_step, emit
    )
    to_natural, to_fine = order[...], spread[...]
    for field in range(3):
        value = result[field].reshape(coarse_rows * 8, half)
        change = value - coarse_before[field].reshape(coarse_rows * 8, half)
        if field == 0:
            value = (result[0] - depth).reshape(coarse_rows * 8, half)
        if field == 2:
            value, change = value * place.sign, change * place.sign
        fine = select(change, to_fine, 2).reshape(coarse_rows, 8, width)
        value = select(value, to_natural, 2).reshape(coarse_rows, 8, half)
        for i in range(coarse_rows):
            store_row(coarse_new, field, coarse_rows, half, place.own_row(coarse_rows, i), value[i])
            for r in (2 * i, 2 * i + 1):
                for c, part in enumerate(tile_slices(rows, width, place.own_row(rows, r))):
                    new_ends[field, part, :] = natural[field, part, :] + fine[i, :, c * LANES : (c + 1) * LANES]


def middle_turn(incoming, near_edge, far_edge, coarse_wet, mean_depth, coupling, place):
    signs = jnp.asarray([1.0, 1.0, -1.0], f32)[:, None, None]
    before = (near_edge * signs).at[0].add((1.0 - place.near_inside) * mean_depth[:, None])
    after = (far_edge * signs).at[0].add((1.0 - place.far_inside) * mean_depth[:, None])
    state = jnp.concatenate([before[:, None], incoming, after[:, None]], axis=1)
    h, u, v = state
    e = h - mean_depth[None, :, None]
    rows, layers, half = incoming.shape[1:]
    blocks = half // LANES
    p = jnp.einsum("kl,rlc->rkc", coupling, e, precision=lax.Precision.HIGHEST)

    def dx_parts(q):
        q = q.reshape(q.shape[0], layers, blocks, LANES)
        east = jnp.concatenate([q[:, :, 1:], jnp.roll(q[:, :, :1], -1, -1)], axis=2)
        west = jnp.concatenate([jnp.roll(q[:, :, -1:], 1, -1), q[:, :, :-1]], axis=2)
        return east.reshape(-1, layers, half)[1:-1], west.reshape(-1, layers, half)[1:-1]

    def dx(q):
        east, west = dx_parts(q)
        return (east - west) / 4.0

    def dy(q):
        return (q[2:] - q[:-2]) / 4.0

    def lap(q):
        east, west = dx_parts(q)
        return (q[2:] + q[:-2] + east + west - 4.0 * q[1:-1]) / 4.0

    um, vm = u[1:-1], v[1:-1]
    f = (place.coarse_first + place.coarse_step * jnp.arange(rows, dtype=f32))[:, None, None] / 4.0
    de = -(dx(h * u) + dy(h * v))
    du = coarse_wet * (-(um * dx(u) + vm * dy(u)) + f * vm - dx(p) + viscosity * lap(u))
    dv = coarse_wet * (-(um * dx(v) + vm * dy(v)) - f * um - dy(p) + viscosity * lap(v))
    return incoming + STEPS * time_step * jnp.stack([de, du, dv])


def local(starts, coarse_old, mean_depth, coupling, wet_cells):
    layers, rows, width = starts.shape[2:]
    coarse_rows, half = rows // 2, width // 2
    assert layers == 8 and rows % 8 == 0 and HALO < rows <= 2 * HALO
    tm, tm_size = lax.axis_index("tm"), lax.axis_size("tm")
    lat_size = lax.axis_size("lat")
    starts = tiles_of(starts[0])
    coarse_old = tiles_of(coarse_old[0])
    vmem = pl.BlockSpec(memory_space=pltpu.VMEM)
    hbm = pl.BlockSpec(memory_space=pltpu.HBM)
    fine_order = interleave_matrix(width)
    coarse_order = interleave_matrix(half)
    planes = 3 * HALO + 2

    def array(*shape):
        return jax.ShapeDtypeStruct(shape, f32)

    def buffer(*shape):
        return pltpu.VMEM(shape, f32)

    def call(kernel, outs, in_specs, scratch=()):
        return pl.pallas_call(
            functools.partial(kernel, rows),
            out_shape=outs,
            in_specs=in_specs,
            out_specs=[vmem] * len(outs),
            scratch_shapes=list(scratch),
            compiler_params=pltpu.CompilerParams(vmem_limit_bytes=16 * 2**20),
        )

    near_of = [i + 1 if i % 2 == 0 else i - 1 for i in range(lat_size)]
    far_of = [i - 1 if i % 2 == 0 else i + 1 for i in range(lat_size)]

    def neighbours(of):
        return [(i, j) for i, j in enumerate(of) if 0 <= j < lat_size]

    to_near, to_far = call(
        pack_kernel,
        [array(planes, 8, width)] * 2,
        [hbm] * 2,
        [
            buffer(*starts.shape),
            pltpu.VMEM((rows, width), jnp.int32),
            buffer(rows, width),
            pltpu.SemaphoreType.DMA((4,)),
        ],
    )(*[pltpu.with_memory_space_constraint(x, pltpu.HBM) for x in (starts, wet_cells)])
    far = lax.ppermute(to_far, "lat", neighbours(far_of))
    near = lax.ppermute(to_near, "lat", neighbours(near_of))
    mean_depths = mean_depth.reshape(1, layers)

    def stage_scratch(count):
        return [buffer(3, count, 8, width)] * 3 + [buffer(count, 8, width)] * 2 + [
            buffer(6, count, 8, width),
            *[pltpu.VMEM((n * 8, 3 * n * 8), bf16) for n in (GROUP, CHUNK)],
        ]

    early_rows, strips, coarse_before, first, coarse_wet = call(
        near_kernel,
        [array(3, rows - HALO, 8, width), array(HALO, 3, 3, 8, width)]
        + [array(3, coarse_rows, 8, half)] * 2
        + [array(coarse_rows, 8, half)],
        [vmem] * 7,
        stage_scratch(HALO + rows),
    )(near, to_near, to_far, coarse_old, mean_depths, coupling, jnp.asarray(coarse_order, bf16))

    late_rows, delta, outcome, passed = call(
        far_kernel,
        [array(3, HALO, 8, width)] + [array(3, coarse_rows, 8, half)] * 3,
        [vmem] * 10,
        stage_scratch(2 * HALO + 1) + [buffer(3, coarse_rows + 2, 8, half)],
    )(far, to_far, near, strips, early_rows, first, coarse_before, coarse_wet, mean_depths, coupling)

    both = ("tm", "lat")

    def hand_on(current):
        def moved(values, of):
            pairs = [
                (t * lat_size + i, (t + 1) * lat_size + j)
                for t in range(tm_size - 1)
                for i, j in enumerate(of)
                if 0 <= j < lat_size
            ]
            return lax.ppermute(values, both, pairs)

        return moved(current, range(lat_size)), moved(current[:, 0], near_of), moved(current[:, -1], far_of)

    previous = outcome
    incoming = hand_on(passed)
    (natural,) = call(natural_kernel, [array(*starts.shape)], [vmem] * 4)(
        early_rows, late_rows, mean_depths, jnp.asarray(fine_order.T, bf16)
    )
    for turn in range(1, tm_size - 1):
        outcome = middle_turn(*incoming, coarse_wet, mean_depth, coupling, Place(rows))
        previous = jnp.where(tm == turn, outcome, previous)
        incoming = hand_on(delta + outcome)

    new_ends, coarse_new = call(
        final_kernel,
        [array(*starts.shape), array(*coarse_old.shape)],
        [vmem] * 11,
        [buffer(3, coarse_rows + 2, 8, half)]
        + [buffer(coarse_rows + 2, 8, half)] * 2
        + [buffer(3, coarse_rows, 8, half)],
    )(
        *incoming, previous, coarse_wet, coarse_before, mean_depths, coupling, natural,
        jnp.asarray(coarse_order.T, bf16), jnp.asarray(prolong_matrix(width), bf16),
    )
    return (
        from_tiles(new_ends, layers, rows, width)[None],
        from_tiles(coarse_new, layers, coarse_rows, half)[None],
    )


def solution(mesh):
    in_specs = (
        P("tm", None, None, "lat", None),
        P("tm", None, None, "lat", None),
        P(),
        P(),
        P("lat", None),
    )
    out_specs = (P("tm", None, None, "lat", None), P("tm", None, None, "lat", None))
    return jax.shard_map(local, mesh=mesh, in_specs=in_specs, out_specs=out_specs, check_vma=False)
```

```python
import functools

import jax
import jax.numpy as jnp
import numpy as np
from jax import lax
from jax.experimental import pallas as pl
from jax.experimental.pallas import tpu as pltpu
from jax.sharding import PartitionSpec as P


STEPS = 4
HALO = 3 * STEPS
NEAR = HALO + 2
GROUP = 6
CHUNK = GROUP + 2
LANES = 128

time_step = 0.15
viscosity = 0.02
rotation = 0.3

STAGE_WEIGHTS = (1.0, 0.25, 2.0 / 3.0)
STAGE_MIX = (None, (0.75, 0.25), (1.0 / 3.0, 2.0 / 3.0))
f32, bf16 = jnp.float32, jnp.bfloat16


def interleave_matrix(width):
    blocks = width // LANES
    place = np.arange(width)
    columns = blocks * (place % LANES) + place // LANES
    return (np.arange(width)[:, None] == columns[None, :]).astype(np.float32)


def prolong_matrix(width):
    half = width // 2
    blocks = half // LANES
    place = np.arange(half)
    columns = blocks * (place % LANES) + place // LANES
    return (columns[:, None] == np.arange(width)[None, :] // 2).astype(np.float32)


def tiles_of(x):
    fields, layers, rows, width = x.shape
    x = x.reshape(fields, layers, rows // 8, 8, width // LANES, LANES).transpose(0, 1, 2, 4, 3, 5)
    return x.reshape(fields, layers * rows * width // LANES, LANES)


def from_tiles(x, layers, rows, width):
    fields = x.shape[0]
    x = x.reshape(fields, layers, rows // 8, width // LANES, 8, LANES).transpose(0, 1, 2, 4, 3, 5)
    return x.reshape(fields, layers, rows, width)


def tile_slices(rows, width, r):
    blocks = width // LANES
    if not isinstance(r, int):
        start = lax.div(r, 8) * (8 * blocks) + lax.rem(r, 8)
    else:
        start = (r // 8) * (8 * blocks) + r % 8
    return [pl.ds(start + 8 * c, 8, stride=rows * blocks) for c in range(blocks)]


def load_row(tiles, field, rows, width, r):
    return jnp.concatenate([tiles[field, part, :] for part in tile_slices(rows, width, r)], axis=1)


def blocks_of(x):
    return [x[:, c : c + LANES] for c in range(0, x.shape[1], LANES)]


def east_west(x):
    blocks = blocks_of(x)
    east = jnp.concatenate(blocks[1:] + [pltpu.roll(blocks[0], LANES - 1, 1)], axis=1)
    west = jnp.concatenate([pltpu.roll(blocks[-1], 1, 1)] + blocks[:-1], axis=1)
    return east, west


def restrict_pair(north, south):
    blocks = blocks_of(north + south)
    return 0.25 * jnp.concatenate([a + b for a, b in zip(blocks[0::2], blocks[1::2])], axis=1)


def split(x, parts):
    found = []
    for _ in range(parts - 1):
        found.append(x.astype(bf16))
        x = x - found[-1].astype(f32)
    return found + [x.astype(bf16)]


def dot(a, b):
    return lax.dot_general(a, b, (((1,), (0,)), ((), ())), preferred_element_type=f32)


def select(x, matrix, parts):
    return sum(dot(part, matrix) for part in split(x, parts))


def select_blocks(x, matrix, parts, block=2 * LANES):
    terms = split(x, parts)
    for c in range(0, matrix.shape[1], block):
        yield c, sum(dot(part, matrix[:, c : c + block]) for part in terms)


def layer_major(place, rows, source_rows):
    repeat = rows // source_rows
    shape = (8 * rows, 8 * source_rows)
    target = lax.broadcasted_iota(jnp.int32, shape, 0)
    source = lax.broadcasted_iota(jnp.int32, shape, 1)
    layer = lax.div(target, rows)
    row = lax.div(place.own_row(rows, target - rows * layer), repeat)
    return jnp.where(source == 8 * row + layer, 1.0, 0.0).astype(bf16)


def reorder(matrix, x, parts=2):
    return sum(dot(matrix, part) for part in split(x, parts))


def coupling_parts(coupling, count):
    size = 8 * count
    high, low = split(jnp.concatenate([coupling] * count, axis=0), 2)
    layer = lax.broadcasted_iota(jnp.int32, (8, 3 * size), 0)
    column = lax.broadcasted_iota(jnp.int32, (8, 3 * size), 1)
    spread = jnp.where((column & 7) == layer, 1.0, 0.0).astype(bf16)
    row = lax.broadcasted_iota(jnp.int32, (size, 3 * size), 0)
    column = lax.broadcasted_iota(jnp.int32, (size, 3 * size), 1)
    third = jnp.where(column >= 2 * size, 2, jnp.where(column >= size, 1, 0))
    parts = jnp.where(third == 2, dot(low, spread), dot(high, spread))
    return jnp.where(((column - size * third) >> 3) == (row >> 3), parts, 0.0).astype(bf16)


def depth_of(mean_depth, width):
    row = lax.broadcasted_iota(jnp.int32, (8, 8), 0)
    column = lax.broadcasted_iota(jnp.int32, (8, 8), 1)
    diagonal = jnp.where(row == column, jnp.broadcast_to(mean_depth[...], (8, 8)), 0.0)
    return select(diagonal, jnp.ones((8, width), bf16), 3)


class Place:
    def __init__(self, rows):
        lat, lat_size = lax.axis_index("lat"), lax.axis_size("lat")
        tm, tm_size = lax.axis_index("tm"), lax.axis_size("tm")
        total = rows * lat_size
        self.even = lax.rem(lat, 2) == 0
        self.last = tm == tm_size - 1
        self.sign = jnp.where(self.even, -1.0, 1.0).astype(f32)
        low, high = (lat > 0).astype(f32), (lat < lat_size - 1).astype(f32)
        self.near_inside = jnp.where(self.even, high, low)
        self.far_inside = jnp.where(self.even, low, high)
        lat_f = lat.astype(f32)
        self.step = 4.0 * rotation / total
        self.coarse_step = 16.0 * rotation / total
        first = self.step * (lat_f * rows + 0.5) - 2.0 * rotation
        coarse = self.coarse_step * (lat_f * (rows // 2) + 0.5) - 4.0 * rotation
        self.first = jnp.where(self.even, -(first + self.step * (rows - 1)), first)
        self.coarse_first = jnp.where(self.even, -(coarse + self.coarse_step * (rows // 2 - 1)), coarse)

    def own_row(self, rows, i):
        return jnp.where(self.even, rows - 1 - i, i)


def pressure_rows(source, hv, press, start, count, kron_parts):
    h = source[0, pl.ds(start, count)]
    hv[pl.ds(start, count)] = h * source[2, pl.ds(start, count)]
    layers, width = h.shape[1:]
    high, low = split(h.reshape(count * layers, width), 2)
    p = dot(kron_parts[count][...], jnp.concatenate([high, low, high], axis=0))
    press[pl.ds(start, count)] = p.reshape(count, layers, width)


def row_tendency(source, hv, press, r, twice_viscosity, coriolis):
    h, u, v = source[0, r], source[1, r], source[2, r]
    u_north, u_south = source[1, r + 1], source[1, r - 1]
    v_north, v_south = source[2, r + 1], source[2, r - 1]
    hu_east, hu_west = east_west(h * u)
    divergence = (hu_east - hu_west) + (hv[r + 1] - hv[r - 1])
    u_east, u_west = east_west(u)
    v_east, v_west = east_west(v)
    p_east, p_west = east_west(press[r])
    to_east, to_west = twice_viscosity - u, twice_viscosity + u
    to_north, to_south = twice_viscosity - v, twice_viscosity + v
    zonal = (to_east * u_east + to_west * u_west) + (to_north * u_north + to_south * u_south)
    zonal = (zonal - (p_east - p_west)) + coriolis * v
    merid = (to_east * v_east + to_west * v_west) + (to_north * v_north + to_south * v_south)
    merid = (merid - (press[r + 1] - press[r - 1])) - coriolis * u
    return (h, u, v), (divergence, zonal, merid)


def run_stage(
    source, target, base, hv, press, wet, low, high, count, which, kron_parts, coriolis_of, inside_of
):
    factor = STAGE_WEIGHTS[which] * time_step / 2.0
    mix = STAGE_MIX[which]

    def one(r):
        here, rates = row_tendency(source, hv, press, r, 2.0 * viscosity, coriolis_of(r))
        mask, keep = wet[which, r], wet[3 + which, r]
        values = [here[0] if mix is None else mix[1] * here[0], keep * here[1], keep * here[2]]
        scales = (-factor * inside_of(r), mask, mask)
        for field in range(3):
            value = values[field]
            if mix is not None:
                value = value + mix[0] * base[field, r]
            target[field, r] = value + scales[field] * rates[field]

    def group(first):
        for i in range(GROUP):
            one(first + i)

    def fill(start, count):
        pressure_rows(source, hv, press, start, count, kron_parts)

    if isinstance(count, int):
        fill(low - 1, GROUP + 2)
        for first in range(0, count, GROUP):
            if first + GROUP < count:
                fill(low + first + GROUP + 1, GROUP)
            group(low + first)
        return

    def turn(k, unused):
        first = low + GROUP * k
        group(first)
        fill(jnp.minimum(first + GROUP + 1, high + 1 - GROUP), GROUP)
        return unused

    def two(k, unused):
        first = high - 2 * (rest - k)
        one(first)
        one(first + 1)
        return unused

    turns = lax.div(count, GROUP)
    rest = lax.div(count - GROUP * turns, 2)
    fill(jnp.minimum(low - 1, high - 1 - GROUP), GROUP + 2)
    lax.fori_loop(0, turns, turn, 0)
    lax.fori_loop(0, rest, two, 0)


def coarse_update(state, hv, press, wet_of, size, rows, kron_parts, coriolis_of, emit, inside=1.0):
    scale = STEPS * time_step / 4.0
    start = 0
    while start < size:
        pressure_rows(state, hv, press, min(start, size - CHUNK), CHUNK, kron_parts)
        start += CHUNK
    for i in rows:
        (h, u, v), (dh, du, dv) = row_tendency(state, hv, press, i, viscosity, coriolis_of(i))
        mask = wet_of(i) * scale
        keep = 1.0 - 4.0 * viscosity * mask
        step = scale * inside if i == rows[0] else scale
        emit(i, (h - step * dh, keep * u + mask * du, keep * v + mask * dv))


def wet_row(halo, count, i):
    plane, row = (0, i) if i < 8 else (1, i - count + 8)
    return halo[3 * count + plane, pl.ds(row, 1), :]


def set_masks(wet, i, mask):
    for which, weight in enumerate(STAGE_WEIGHTS):
        scaled = mask * (weight * time_step / 2.0)
        wet[which, i] = scaled
        wet[3 + which, i] = weight - 8.0 * viscosity * scaled


def turned(x, field):
    return -x if field == 2 else x


def pack_kernel(
    rows, starts_hbm, wet_hbm, coarse_hbm, coupling_hbm, depth_hbm, order_hbm,
    to_near, to_far, coarse_old, coupling, mean_depth, coarse_order,
    starts, wet_cells, wet, semaphores,
):
    width = wet_cells.shape[-1]
    blocks = width // LANES
    pairs = [(starts_hbm.at[field], starts.at[field]) for field in range(3)] + [(wet_hbm, wet_cells)]
    pairs += [(coarse_hbm, coarse_old), (coupling_hbm, coupling), (depth_hbm, mean_depth), (order_hbm, coarse_order)]
    copies = [pltpu.make_async_copy(source, target, semaphores.at[n]) for n, (source, target) in enumerate(pairs)]
    for copy in copies:
        copy.start()
    place = Place(rows)
    column = lax.broadcasted_iota(jnp.int32, (width, LANES), 0)
    column = column - blocks * lax.broadcasted_iota(jnp.int32, (width, LANES), 1)
    order = jnp.concatenate([jnp.where(column == c, 1.0, 0.0).astype(bf16) for c in range(blocks)], axis=1)
    sent = ((to_near, 0, NEAR), (to_far, rows - HALO, HALO))
    for field in range(3):
        copies[field].wait()
        state = [load_row(starts, field, rows, width, place.own_row(rows, i)) for i in range(rows)]
        state = jnp.concatenate(state, axis=0)
        for c, value in select_blocks(state * place.sign if field == 2 else state, order, 2):
            value = value.reshape(rows, 8, value.shape[1])
            for packed, first, count in sent:
                packed[field * count : (field + 1) * count, :, c : c + value.shape[2]] = value[first : first + count]
    copies[3].wait()
    wet[...] = dot(wet_cells[...].astype(f32).astype(bf16), order)
    for packed, first, count in sent:
        for plane, skip in ((0, 0), (1, count - 8)):
            if plane == 0 or count > 8:
                for i in range(min(8, count)):
                    row = place.own_row(rows, first + skip + i)
                    packed[3 * count + plane, pl.ds(i, 1), :] = wet[pl.ds(row, 1), :]
    for copy in copies[4:]:
        copy.wait()
    half = width // 2
    old = [load_row(coarse_old, field, rows // 2, half, place.own_row(rows // 2, 0)) for field in range(3)]
    old[2] = old[2] * place.sign
    old = select(jnp.concatenate(old, axis=0), coarse_order[...], 2)
    to_near[3 * NEAR + 2, :, :half] = old[:8]
    to_near[3 * NEAR + 2, :, half:] = old[8:16]
    to_near[3 * NEAR + 3, :, :half] = old[16:]
    to_near[3 * NEAR + 3, :, half:] = old[16:]


def near_kernel(
    rows, near, to_near, to_far, coarse_old, mean_depth, coupling, matrix,
    early_rows, strips, coarse_before, first, outcome, coarse_wet,
    y, a, b, hv, press, wet, short_parts, long_parts,
):
    width = y.shape[-1]
    half = width // 2
    coarse_rows = rows // 2
    place = Place(rows)
    depth = depth_of(mean_depth, width)
    kron_parts = {}
    for count, parts in ((GROUP, short_parts), (CHUNK, long_parts)):
        parts[...] = coupling_parts(coupling[...], count)
        kron_parts[count] = parts
    for i in range(NEAR):
        for field in range(3):
            value = turned(near[field * NEAR + i], field)
            y[field, NEAR - 1 - i] = value + depth if field == 0 else value
        set_masks(wet, NEAR - 1 - i, jnp.broadcast_to(wet_row(near, NEAR, i), (8, width)))
    for i in range(rows):
        sent, at, count = (to_near, i, NEAR) if i < NEAR else (to_far, i - rows + HALO, HALO)
        for field in range(3):
            value = sent[field * count + at]
            y[field, NEAR + i] = value + depth if field == 0 else value
        set_masks(wet, NEAR + i, jnp.broadcast_to(wet_row(sent, count, at), (8, width)))

    def keep(state, t):
        for field in range(3):
            strips[t, field] = state[field, pl.ds(NEAR + rows - 3 - t, 3)]

    keep(y, 0)

    for i in range(coarse_rows + 2):
        at = NEAR - 4 + 2 * i
        both = wet[0, at] * wet[0, at + 1]
        blocks = blocks_of(jnp.where(both > 0.0, 1.0, 0.0))
        coarse_wet[i] = jnp.concatenate([p * q for p, q in zip(blocks[0::2], blocks[1::2])], axis=1)
        for field in range(3):
            first[field, i] = restrict_pair(y[field, at], y[field, at + 1])

    def emit(i, values):
        for field in range(3):
            outcome[field, i - 1] = values[field]

    coarse_update(
        first, hv.at[:, :, pl.ds(0, half)], press.at[:, :, pl.ds(0, half)], lambda i: coarse_wet[i],
        coarse_rows + 2, range(1, coarse_rows + 1), kron_parts,
        lambda i: place.coarse_first + place.coarse_step * (i - 2), emit, place.near_inside,
    )
    order = matrix[...]
    arrived = ((3 * NEAR + 2, 0), (3 * NEAR + 2, half), (3 * NEAR + 3, 0))
    for field in range(3):
        old = [
            load_row(coarse_old, field, coarse_rows, half, place.own_row(coarse_rows, i))
            for i in range(coarse_rows)
        ]
        old = select(jnp.concatenate(old, axis=0), order, 2).reshape(coarse_rows, 8, half)
        plane, at = arrived[field]
        edge = turned(near[plane, :, at : at + half], field)
        if field == 0:
            old, edge = old + depth[:, :half], edge + depth[:, :half]
        coarse_before[field, 0] = edge
        coarse_before[field, 1:] = old * place.sign if field == 2 else old

    def coriolis_of(r):
        return place.first + place.step * (r - NEAR).astype(f32)

    def inside_of(r):
        return jnp.where(r < NEAR, place.near_inside, 1.0)

    def step(k, unused):
        for which, (source, target) in enumerate(((y, a), (a, b), (b, y))):
            s = 3 * k + which + 1
            run_stage(
                source, target, y, hv, press, wet, s, NEAR + rows - s, NEAR + rows - 2 * s, which, kron_parts,
                coriolis_of, inside_of,
            )

            @pl.when(s < HALO)
            def _():
                keep(target, s)

        return unused

    lax.fori_loop(0, STEPS, step, 0)
    for field in range(3):
        early_rows[field] = y[field, NEAR - 2 : NEAR + rows - HALO]


def far_kernel(
    rows, far, to_far, strips, early_rows, first, outcome, coarse_before, coarse_wet, mean_depth, coupling,
    late_rows, delta, last_outcome, passed,
    y, a, b, hv, press, wet, short_parts, long_parts, state,
):
    width = y.shape[-1]
    origin = rows - HALO - 1
    own = rows - origin
    coarse_rows = rows // 2
    place = Place(rows)
    depth = depth_of(mean_depth, width)
    kron_parts = {}
    for count, parts in ((GROUP, short_parts), (CHUNK, long_parts)):
        parts[...] = coupling_parts(coupling[...], count)
        kron_parts[count] = parts
    for field in range(3):
        for i in range(HALO):
            value = turned(far[(field + 1) * HALO - 1 - i], field)
            y[field, own + i] = value + depth if field == 0 else value
        state[field, : coarse_rows - 1] = first[field, 3:]
    for i in range(HALO):
        set_masks(wet, own + i, jnp.broadcast_to(wet_row(far, HALO, HALO - 1 - i), (8, width)))
        set_masks(wet, own - HALO + i, jnp.broadcast_to(wet_row(to_far, HALO, i), (8, width)))

    for field in range(3):
        state[field, coarse_rows - 1] = restrict_pair(y[field, own], y[field, own + 1])

    def emit(i, values):
        for field in range(3):
            last_outcome[field] = values[field]

    half = width // 2
    coarse_update(
        state, hv.at[:, :, pl.ds(0, half)], press.at[:, :, pl.ds(0, half)], lambda i: coarse_wet[coarse_rows + 1],
        coarse_rows, [coarse_rows - 2], kron_parts,
        lambda i: place.coarse_first + place.coarse_step * (coarse_rows - 1), emit,
    )

    def coriolis_of(r):
        return place.first + place.step * (r + origin).astype(f32)

    def inside_of(r):
        return jnp.where(r < own, 1.0, place.far_inside)

    def step(k, unused):
        for which, (source, target) in enumerate(((y, a), (a, b), (b, y))):
            t = 3 * k + which
            s = t + 1
            for field in range(3):
                for i in range(0 if which == 0 else 1, 3):
                    source[field, own - 3 - t + i] = strips[t, field, i]
            low = own - s
            run_stage(
                source, target, y, hv, press, wet, low, low + HALO, HALO, which, kron_parts, coriolis_of, inside_of
            )
        return unused

    lax.fori_loop(0, STEPS, step, 0)
    early = rows - HALO
    for field in range(3):
        late_rows[field] = y[field, own - HALO : own]
        for i in range(-1, coarse_rows):
            if 2 * i < early:
                pair = early_rows[field, 2 * i + 2], early_rows[field, 2 * i + 3]
            else:
                pair = y[field, 2 * i - origin], y[field, 2 * i + 1 - origin]
            difference = restrict_pair(*pair) - coarse_before[field, i + 1]
            delta[field, i + 1] = difference
            before = last_outcome[field] if i == coarse_rows - 1 else outcome[field, i + 1]
            passed[field, i + 1] = difference + before


def natural_kernel(rows, early_rows, late_rows, mean_depth, matrix, natural):
    width = late_rows.shape[-1]
    place = Place(rows)
    depth = depth_of(mean_depth, width)
    for field in range(3):
        value = jnp.concatenate([part[field] for part in (early_rows.at[:, 2:], late_rows)], axis=0)
        if field == 0:
            value = value - depth
        if field == 2:
            value = value * place.sign
        for c, piece in select_blocks(value.reshape(rows * 8, width), matrix, 2):
            piece = piece.reshape(rows, 8, piece.shape[1])
            for r in range(rows):
                slices = tile_slices(rows, width, place.own_row(rows, r))
                for at in range(0, piece.shape[2], LANES):
                    natural[field, slices[(c + at) // LANES], :] = piece[r, :, at : at + LANES]


def final_kernel(
    rows, incoming, far_edge, previous, last_previous, coarse_wet, coarse_before, mean_depth, coupling, natural, order,
    spread,
    new_ends, coarse_new,
    state, hv, press, result, ends, coarse, semaphores,
):
    coarse_rows = rows // 2
    half = incoming.shape[-1]
    width = 2 * half
    place = Place(rows)
    depth = depth_of(mean_depth, half)
    for field in range(3):
        state[field, : coarse_rows + 1] = incoming[field]
        state[field, coarse_rows + 1] = turned(far_edge[field], field)
    state[0, coarse_rows + 1] += (1.0 - place.far_inside) * depth
    kron_parts = {CHUNK: coupling_parts(coupling[...], CHUNK)}

    def emit(i, values):
        for field in range(3):
            before = last_previous[field] if i == coarse_rows else previous[field, i]
            result[field, i - 1] = jnp.where(place.last, values[field], before)

    coarse_update(
        state, hv, press, lambda i: coarse_wet[i + 1], coarse_rows + 2, range(1, coarse_rows + 1), kron_parts,
        lambda i: place.coarse_first + place.coarse_step * (i - 1), emit,
    )
    to_natural = order[...]
    fine_rows = layer_major(place, rows, coarse_rows)
    own_rows = layer_major(place, coarse_rows, coarse_rows)
    copies = []
    for field in range(3):
        value = result[field].reshape(coarse_rows * 8, half)
        change = value - coarse_before[field, 1:].reshape(coarse_rows * 8, half)
        if field == 0:
            value = (result[0] - depth).reshape(coarse_rows * 8, half)
        if field == 2:
            value, change = value * place.sign, change * place.sign
        value = select(reorder(own_rows, value), to_natural, 2)
        for k in range(coarse_rows):
            for c in range(half // LANES):
                tile = pl.ds((k * (half // LANES) + c) * 8, 8)
                coarse[field, tile, :] = value[8 * k : 8 * k + 8, c * LANES : (c + 1) * LANES]
        copies.append(pltpu.make_async_copy(coarse.at[field], coarse_new.at[field], semaphores.at[3 + field]))
        copies[-1].start()
        for c, fine in select_blocks(reorder(fine_rows, change), spread, 2):
            for k in range(8 * rows // 8):
                for at in range(0, fine.shape[1], LANES):
                    tile = pl.ds((k * (width // LANES) + (c + at) // LANES) * 8, 8)
                    ends[field, tile, :] = natural[field, tile, :] + fine[8 * k : 8 * k + 8, at : at + LANES]
        copies.append(pltpu.make_async_copy(ends.at[field], new_ends.at[field], semaphores.at[field]))
        copies[-1].start()
    for copy in copies:
        copy.wait()


def middle_turn(incoming, far_edge, coarse_wet, mean_depth, coupling, place):
    signs = jnp.asarray([1.0, 1.0, -1.0], f32)[:, None, None]
    after = (far_edge * signs).at[0].add((1.0 - place.far_inside) * mean_depth[:, None])
    state = jnp.concatenate([incoming, after[:, None]], axis=1)
    incoming = incoming[:, 1:]
    h, u, v = state
    e = h - mean_depth[None, :, None]
    rows, layers, half = incoming.shape[1:]
    blocks = half // LANES
    p = jnp.einsum("kl,rlc->rkc", coupling, e, precision=lax.Precision.HIGHEST)

    def dx_parts(q):
        q = q.reshape(q.shape[0], layers, blocks, LANES)
        east = jnp.concatenate([q[:, :, 1:], jnp.roll(q[:, :, :1], -1, -1)], axis=2)
        west = jnp.concatenate([jnp.roll(q[:, :, -1:], 1, -1), q[:, :, :-1]], axis=2)
        return east.reshape(-1, layers, half)[1:-1], west.reshape(-1, layers, half)[1:-1]

    def dx(q):
        east, west = dx_parts(q)
        return (east - west) / 4.0

    def dy(q):
        return (q[2:] - q[:-2]) / 4.0

    def lap(q):
        east, west = dx_parts(q)
        return (q[2:] + q[:-2] + east + west - 4.0 * q[1:-1]) / 4.0

    um, vm = u[1:-1], v[1:-1]
    f = (place.coarse_first + place.coarse_step * jnp.arange(rows, dtype=f32))[:, None, None] / 4.0
    de = -(dx(h * u) + dy(h * v))
    du = coarse_wet * (-(um * dx(u) + vm * dy(u)) + f * vm - dx(p) + viscosity * lap(u))
    dv = coarse_wet * (-(um * dx(v) + vm * dy(v)) - f * um - dy(p) + viscosity * lap(v))
    return incoming + STEPS * time_step * jnp.stack([de, du, dv])


def local(starts, coarse_old, mean_depth, coupling, wet_cells):
    layers, rows, width = starts.shape[2:]
    coarse_rows, half = rows // 2, width // 2
    assert layers == 8 and rows % 8 == 0 and NEAR <= rows <= 2 * HALO
    tm, tm_size = lax.axis_index("tm"), lax.axis_size("tm")
    lat_size = lax.axis_size("lat")
    starts = tiles_of(starts[0])
    coarse_old = tiles_of(coarse_old[0])
    vmem = pl.BlockSpec(memory_space=pltpu.VMEM)
    hbm = pl.BlockSpec(memory_space=pltpu.HBM)
    fine_order = interleave_matrix(width)
    coarse_order = interleave_matrix(half)

    def array(*shape):
        return jax.ShapeDtypeStruct(shape, f32)

    def buffer(*shape):
        return pltpu.VMEM(shape, f32)

    def call(kernel, outs, in_specs, scratch=(), out_specs=None):
        return pl.pallas_call(
            functools.partial(kernel, rows),
            out_shape=outs,
            in_specs=in_specs,
            out_specs=out_specs or [vmem] * len(outs),
            scratch_shapes=list(scratch),
            compiler_params=pltpu.CompilerParams(vmem_limit_bytes=16 * 2**20),
        )

    near_of = [i + 1 if i % 2 == 0 else i - 1 for i in range(lat_size)]
    far_of = [i - 1 if i % 2 == 0 else i + 1 for i in range(lat_size)]

    def neighbours(of):
        return [(i, j) for i, j in enumerate(of) if 0 <= j < lat_size]

    operands = (
        starts, wet_cells, coarse_old, coupling, mean_depth.reshape(1, layers), jnp.asarray(coarse_order, bf16)
    )
    to_near, to_far, coarse_old, coupling_kept, mean_depths, order = call(
        pack_kernel,
        [array(3 * NEAR + 4, 8, width), array(3 * HALO + 2, 8, width)]
        + [jax.ShapeDtypeStruct(x.shape, x.dtype) for x in operands[2:]],
        [hbm] * 6,
        [
            buffer(*starts.shape),
            pltpu.VMEM((rows, width), jnp.int32),
            buffer(rows, width),
            pltpu.SemaphoreType.DMA((8,)),
        ],
    )(*[pltpu.with_memory_space_constraint(x, pltpu.HBM) for x in operands])
    far = lax.ppermute(to_far, "lat", neighbours(far_of))
    near = lax.ppermute(to_near, "lat", neighbours(near_of))

    def stage_scratch(count):
        return [buffer(3, count, 8, width)] * 3 + [buffer(count, 8, width)] * 2 + [
            buffer(6, count, 8, width),
            *[pltpu.VMEM((n * 8, 3 * n * 8), bf16) for n in (GROUP, CHUNK)],
        ]

    early_rows, strips, coarse_before, first, outcome, coarse_wet = call(
        near_kernel,
        [array(3, rows - HALO + 2, 8, width), array(HALO, 3, 3, 8, width)]
        + [array(3, coarse_rows + n, 8, half) for n in (1, 2, 0)]
        + [array(coarse_rows + 2, 8, half)],
        [vmem] * 7,
        stage_scratch(NEAR + rows),
    )(near, to_near, to_far, coarse_old, mean_depths, coupling_kept, order)

    late_rows, delta, last_outcome, passed = call(
        far_kernel,
        [array(3, HALO, 8, width), array(3, coarse_rows + 1, 8, half), array(3, 8, half)]
        + [array(3, coarse_rows + 1, 8, half)],
        [vmem] * 10,
        stage_scratch(2 * HALO + 1) + [buffer(3, coarse_rows, 8, half)],
    )(far, to_far, strips, early_rows, first, outcome, coarse_before, coarse_wet, mean_depths, coupling_kept)

    both = ("tm", "lat")

    def hand_on(current):
        def moved(values, of):
            pairs = [
                (t * lat_size + i, (t + 1) * lat_size + j)
                for t in range(tm_size - 1)
                for i, j in enumerate(of)
                if 0 <= j < lat_size
            ]
            return lax.ppermute(values, both, pairs)

        main, far_edge = moved(current, range(lat_size)), moved(current[:, -1], far_of)
        if current.shape[1] > coarse_rows:
            return main, far_edge
        near_edge = moved(current[:, 0], near_of) * jnp.asarray([1.0, 1.0, -1.0], f32)[:, None, None]
        near_edge = near_edge.at[0].add((1.0 - Place(rows).near_inside) * mean_depth[:, None])
        return jnp.concatenate([near_edge[:, None], main], axis=1), far_edge

    previous, last_previous = outcome, last_outcome
    incoming = hand_on(passed)
    (natural,) = call(natural_kernel, [array(*starts.shape)], [vmem] * 4)(
        early_rows, late_rows, mean_depths, jnp.asarray(fine_order.T, bf16)
    )
    for turn in range(1, tm_size - 1):
        result = middle_turn(*incoming, coarse_wet[2:], mean_depth, coupling, Place(rows))
        previous = jnp.where(tm == turn, jnp.concatenate([previous[:, :1], result[:, :-1]], axis=1), previous)
        last_previous = jnp.where(tm == turn, result[:, -1], last_previous)
        incoming = hand_on(delta[:, 1:] + result)

    new_ends, coarse_new = call(
        final_kernel,
        [array(*starts.shape), array(*coarse_old.shape)],
        [vmem] * 11,
        [buffer(3, coarse_rows + 2, 8, half)]
        + [buffer(coarse_rows + 2, 8, half)] * 2
        + [buffer(3, coarse_rows, 8, half), buffer(*starts.shape), buffer(*coarse_old.shape)]
        + [pltpu.SemaphoreType.DMA((6,))],
        [hbm, hbm],
    )(
        *incoming, previous, last_previous, coarse_wet, coarse_before, mean_depths, coupling_kept, natural,
        jnp.asarray(coarse_order.T, bf16), jnp.asarray(prolong_matrix(width), bf16),
    )
    return (
        from_tiles(new_ends, layers, rows, width)[None],
        from_tiles(coarse_new, layers, coarse_rows, half)[None],
    )


def solution(mesh):
    in_specs = (
        P("tm", None, None, "lat", None),
        P("tm", None, None, "lat", None),
        P(),
        P(),
        P("lat", None),
    )
    out_specs = (P("tm", None, None, "lat", None), P("tm", None, None, "lat", None))
    return jax.shard_map(local, mesh=mesh, in_specs=in_specs, out_specs=out_specs, check_vma=False)
```

```python
import functools

import jax
import jax.numpy as jnp
import numpy as np
from jax import lax
from jax.experimental import pallas as pl
from jax.experimental.pallas import tpu as pltpu
from jax.sharding import PartitionSpec as P


STEPS = 4
HALO = 3 * STEPS
NEAR = HALO + 2
GROUP = 6
CHUNK = GROUP + 2
LANES = 128

time_step = 0.15
viscosity = 0.02
rotation = 0.3

STAGE_WEIGHTS = (1.0, 0.25, 2.0 / 3.0)
STAGE_MIX = (None, (0.75, 0.25), (1.0 / 3.0, 2.0 / 3.0))
f32, bf16 = jnp.float32, jnp.bfloat16


def interleave_matrix(width):
    blocks = width // LANES
    place = np.arange(width)
    columns = blocks * (place % LANES) + place // LANES
    return (np.arange(width)[:, None] == columns[None, :]).astype(np.float32)


def prolong_matrix(width):
    half = width // 2
    blocks = half // LANES
    place = np.arange(half)
    columns = blocks * (place % LANES) + place // LANES
    return (columns[:, None] == np.arange(width)[None, :] // 2).astype(np.float32)


def tiles_of(x):
    fields, layers, rows, width = x.shape
    x = x.reshape(fields, layers, rows // 8, 8, width // LANES, LANES).transpose(0, 1, 2, 4, 3, 5)
    return x.reshape(fields, layers * rows * width // LANES, LANES)


def from_tiles(x, layers, rows, width):
    fields = x.shape[0]
    x = x.reshape(fields, layers, rows // 8, width // LANES, 8, LANES).transpose(0, 1, 2, 4, 3, 5)
    return x.reshape(fields, layers, rows, width)


def tile_slices(rows, width, r):
    blocks = width // LANES
    if not isinstance(r, int):
        start = lax.div(r, 8) * (8 * blocks) + lax.rem(r, 8)
    else:
        start = (r // 8) * (8 * blocks) + r % 8
    return [pl.ds(start + 8 * c, 8, stride=rows * blocks) for c in range(blocks)]


def load_row(tiles, field, rows, width, r):
    return jnp.concatenate([tiles[field, part, :] for part in tile_slices(rows, width, r)], axis=1)


def blocks_of(x):
    return [x[:, c : c + LANES] for c in range(0, x.shape[1], LANES)]


def east_west(x):
    blocks = blocks_of(x)
    east = jnp.concatenate(blocks[1:] + [pltpu.roll(blocks[0], LANES - 1, 1)], axis=1)
    west = jnp.concatenate([pltpu.roll(blocks[-1], 1, 1)] + blocks[:-1], axis=1)
    return east, west


def restrict_pair(north, south):
    blocks = blocks_of(north + south)
    return 0.25 * jnp.concatenate([a + b for a, b in zip(blocks[0::2], blocks[1::2])], axis=1)


def split(x, parts):
    found = []
    for _ in range(parts - 1):
        found.append(x.astype(bf16))
        x = x - found[-1].astype(f32)
    return found + [x.astype(bf16)]


def dot(a, b):
    return lax.dot_general(a, b, (((1,), (0,)), ((), ())), preferred_element_type=f32)


def select(x, matrix, parts):
    return sum(dot(part, matrix) for part in split(x, parts))


def select_blocks(x, matrix, parts, block=2 * LANES):
    terms = split(x, parts)
    for c in range(0, matrix.shape[1], block):
        yield c, sum(dot(part, matrix[:, c : c + block]) for part in terms)


def layer_major(place, rows, source_rows):
    repeat = rows // source_rows
    shape = (8 * rows, 8 * source_rows)
    target = lax.broadcasted_iota(jnp.int32, shape, 0)
    source = lax.broadcasted_iota(jnp.int32, shape, 1)
    layer = lax.div(target, rows)
    row = lax.div(place.own_row(rows, target - rows * layer), repeat)
    return jnp.where(source == 8 * row + layer, 1.0, 0.0).astype(bf16)


def reorder(matrix, x, parts=2):
    return sum(dot(matrix, part) for part in split(x, parts))


def coupling_parts(coupling, count):
    size = 8 * count
    high, low = split(jnp.concatenate([coupling] * count, axis=0), 2)
    layer = lax.broadcasted_iota(jnp.int32, (8, 3 * size), 0)
    column = lax.broadcasted_iota(jnp.int32, (8, 3 * size), 1)
    spread = jnp.where((column & 7) == layer, 1.0, 0.0).astype(bf16)
    row = lax.broadcasted_iota(jnp.int32, (size, 3 * size), 0)
    column = lax.broadcasted_iota(jnp.int32, (size, 3 * size), 1)
    third = jnp.where(column >= 2 * size, 2, jnp.where(column >= size, 1, 0))
    parts = jnp.where(third == 2, dot(low, spread), dot(high, spread))
    return jnp.where(((column - size * third) >> 3) == (row >> 3), parts, 0.0).astype(bf16)


def depth_of(mean_depth, width):
    row = lax.broadcasted_iota(jnp.int32, (8, 8), 0)
    column = lax.broadcasted_iota(jnp.int32, (8, 8), 1)
    diagonal = jnp.where(row == column, jnp.broadcast_to(mean_depth[...], (8, 8)), 0.0)
    return select(diagonal, jnp.ones((8, width), bf16), 3)


class Place:
    def __init__(self, rows):
        lat, lat_size = lax.axis_index("lat"), lax.axis_size("lat")
        tm, tm_size = lax.axis_index("tm"), lax.axis_size("tm")
        total = rows * lat_size
        self.even = lax.rem(lat, 2) == 0
        self.last = tm == tm_size - 1
        self.sign = jnp.where(self.even, -1.0, 1.0).astype(f32)
        low, high = (lat > 0).astype(f32), (lat < lat_size - 1).astype(f32)
        self.near_inside = jnp.where(self.even, high, low)
        self.far_inside = jnp.where(self.even, low, high)
        lat_f = lat.astype(f32)
        self.step = 4.0 * rotation / total
        self.coarse_step = 16.0 * rotation / total
        first = self.step * (lat_f * rows + 0.5) - 2.0 * rotation
        coarse = self.coarse_step * (lat_f * (rows // 2) + 0.5) - 4.0 * rotation
        self.first = jnp.where(self.even, -(first + self.step * (rows - 1)), first)
        self.coarse_first = jnp.where(self.even, -(coarse + self.coarse_step * (rows // 2 - 1)), coarse)

    def own_row(self, rows, i):
        return jnp.where(self.even, rows - 1 - i, i)


def pressure_rows(source, hv, press, start, count, kron_parts):
    h = source[0, pl.ds(start, count)]
    hv[pl.ds(start, count)] = h * source[2, pl.ds(start, count)]
    layers, width = h.shape[1:]
    high, low = split(h.reshape(count * layers, width), 2)
    p = dot(kron_parts[count][...], jnp.concatenate([high, low, high], axis=0))
    press[pl.ds(start, count)] = p.reshape(count, layers, width)


def row_tendency(source, hv, press, r, twice_viscosity, coriolis):
    h, u, v = source[0, r], source[1, r], source[2, r]
    u_north, u_south = source[1, r + 1], source[1, r - 1]
    v_north, v_south = source[2, r + 1], source[2, r - 1]
    hu_east, hu_west = east_west(h * u)
    divergence = (hu_east - hu_west) + (hv[r + 1] - hv[r - 1])
    u_east, u_west = east_west(u)
    v_east, v_west = east_west(v)
    p_east, p_west = east_west(press[r])
    to_east, to_west = twice_viscosity - u, twice_viscosity + u
    to_north, to_south = twice_viscosity - v, twice_viscosity + v
    zonal = (to_east * u_east + to_west * u_west) + (to_north * u_north + to_south * u_south)
    zonal = (zonal - (p_east - p_west)) + coriolis * v
    merid = (to_east * v_east + to_west * v_west) + (to_north * v_north + to_south * v_south)
    merid = (merid - (press[r + 1] - press[r - 1])) - coriolis * u
    return (h, u, v), (divergence, zonal, merid)


def run_stage(
    source, target, base, hv, press, wet, low, high, count, which, kron_parts, coriolis_of, inside_of
):
    factor = STAGE_WEIGHTS[which] * time_step / 2.0
    mix = STAGE_MIX[which]

    def one(r):
        here, rates = row_tendency(source, hv, press, r, 2.0 * viscosity, coriolis_of(r))
        mask, keep = wet[which, r], wet[3 + which, r]
        values = [here[0] if mix is None else mix[1] * here[0], keep * here[1], keep * here[2]]
        scales = (-factor * inside_of(r), mask, mask)
        for field in range(3):
            value = values[field]
            if mix is not None:
                value = value + mix[0] * base[field, r]
            target[field, r] = value + scales[field] * rates[field]

    def group(first):
        for i in range(GROUP):
            one(first + i)

    def fill(start, count):
        pressure_rows(source, hv, press, start, count, kron_parts)

    if isinstance(count, int):
        fill(low - 1, GROUP + 2)
        for first in range(0, count, GROUP):
            if first + GROUP < count:
                fill(low + first + GROUP + 1, GROUP)
            group(low + first)
        return

    def turn(k, unused):
        first = low + GROUP * k
        group(first)
        fill(jnp.minimum(first + GROUP + 1, high + 1 - GROUP), GROUP)
        return unused

    def two(k, unused):
        first = high - 2 * (rest - k)
        one(first)
        one(first + 1)
        return unused

    turns = lax.div(count, GROUP)
    rest = lax.div(count - GROUP * turns, 2)
    fill(jnp.minimum(low - 1, high - 1 - GROUP), GROUP + 2)
    lax.fori_loop(0, turns, turn, 0)
    lax.fori_loop(0, rest, two, 0)


def coarse_update(state, hv, press, wet_of, size, rows, kron_parts, coriolis_of, emit, inside=1.0):
    scale = STEPS * time_step / 4.0
    start = 0
    while start < size:
        pressure_rows(state, hv, press, min(start, size - CHUNK), CHUNK, kron_parts)
        start += CHUNK
    for i in rows:
        (h, u, v), (dh, du, dv) = row_tendency(state, hv, press, i, viscosity, coriolis_of(i))
        mask = wet_of(i) * scale
        keep = 1.0 - 4.0 * viscosity * mask
        step = scale * inside if i == rows[0] else scale
        emit(i, (h - step * dh, keep * u + mask * du, keep * v + mask * dv))


def wet_row(halo, count, i):
    plane, row = (0, i) if i < 8 else (1, i - count + 8)
    return halo[3 * count + plane, pl.ds(row, 1), :]


def set_masks(wet, i, mask):
    for which, weight in enumerate(STAGE_WEIGHTS):
        scaled = mask * (weight * time_step / 2.0)
        wet[which, i] = scaled
        wet[3 + which, i] = weight - 8.0 * viscosity * scaled


def turned(x, field):
    return -x if field == 2 else x


def order_of(width):
    blocks = width // LANES
    column = lax.broadcasted_iota(jnp.int32, (width, LANES), 0)
    column = column - blocks * lax.broadcasted_iota(jnp.int32, (width, LANES), 1)
    return jnp.concatenate([jnp.where(column == c, 1.0, 0.0).astype(bf16) for c in range(blocks)], axis=1)


def packed_rows(place, starts, order, rows, width, chosen):
    state = [
        load_row(starts, field, rows, width, place.own_row(rows, i)) * (place.sign if field == 2 else 1.0)
        for field in range(3)
        for i in chosen
    ]
    count = 8 * len(state)
    terms = jnp.concatenate(split(jnp.concatenate(state, axis=0), 2), axis=0)
    for c in range(0, width, 2 * LANES):
        value = dot(terms, order[:, c : c + 2 * LANES])
        yield c, (value[:count] + value[count:]).reshape(3, len(chosen), 8, 2 * LANES)


def pack_wet(place, packed, wet, rows, first, count):
    for plane, skip in ((0, 0), (1, count - 8)):
        for i in range(8):
            row = place.own_row(rows, first + skip + i)
            packed[3 * count + plane, pl.ds(i, 1), :] = wet[pl.ds(row, 1), :]


def pack_far_kernel(rows, starts_hbm, wet_hbm, to_far, starts, order, wet, wet_cells, semaphores):
    width = wet_cells.shape[-1]
    pairs = [(starts_hbm.at[field], starts.at[field]) for field in range(3)] + [(wet_hbm, wet_cells)]
    copies = [pltpu.make_async_copy(source, target, semaphores.at[n]) for n, (source, target) in enumerate(pairs)]
    for copy in copies:
        copy.start()
    place = Place(rows)
    order[...] = order_of(width)
    for copy in copies:
        copy.wait()
    for c, value in packed_rows(place, starts, order, rows, width, range(rows - HALO, rows)):
        for field in range(3):
            to_far[field * HALO : (field + 1) * HALO, :, c : c + value.shape[3]] = value[field]
    wet[...] = dot(wet_cells[...].astype(f32).astype(bf16), order[...])
    pack_wet(place, to_far, wet, rows, rows - HALO, HALO)


def pack_near_kernel(
    rows, starts, order, wet, to_far, coarse_hbm, coupling_hbm, depth_hbm, order_hbm,
    to_near, coarse_old, coupling, mean_depth, coarse_order,
    semaphores,
):
    width = wet.shape[-1]
    pairs = [(coarse_hbm, coarse_old), (coupling_hbm, coupling), (depth_hbm, mean_depth), (order_hbm, coarse_order)]
    copies = [pltpu.make_async_copy(source, target, semaphores.at[n]) for n, (source, target) in enumerate(pairs)]
    for copy in copies:
        copy.start()
    place = Place(rows)
    early = rows - HALO
    for c, value in packed_rows(place, starts, order, rows, width, range(early)):
        for field in range(3):
            to_near[field * NEAR : field * NEAR + early, :, c : c + value.shape[3]] = value[field]
    for field in range(3):
        to_near[field * NEAR + early : (field + 1) * NEAR] = to_far[field * HALO : field * HALO + NEAR - early]
    pack_wet(place, to_near, wet, rows, 0, NEAR)
    for copy in copies:
        copy.wait()
    half = width // 2
    old = [load_row(coarse_old, field, rows // 2, half, place.own_row(rows // 2, 0)) for field in range(3)]
    old[2] = old[2] * place.sign
    old = select(jnp.concatenate(old, axis=0), coarse_order[...], 2)
    to_near[3 * NEAR + 2, :, :half] = old[:8]
    to_near[3 * NEAR + 2, :, half:] = old[8:16]
    to_near[3 * NEAR + 3, :, :half] = old[16:]
    to_near[3 * NEAR + 3, :, half:] = old[16:]


def near_kernel(
    rows, near, to_near, to_far, coarse_old, mean_depth, coupling, matrix,
    early_rows, strips, coarse_before, first, outcome, coarse_wet, short_parts, long_parts, depths,
    y, a, b, hv, press, wet,
):
    width = y.shape[-1]
    half = width // 2
    coarse_rows = rows // 2
    place = Place(rows)
    depth = depth_of(mean_depth, width)
    depths[...] = depth
    kron_parts = {}
    for count, parts in ((GROUP, short_parts), (CHUNK, long_parts)):
        parts[...] = coupling_parts(coupling[...], count)
        kron_parts[count] = parts
    for i in range(NEAR):
        for field in range(3):
            value = turned(near[field * NEAR + i], field)
            y[field, NEAR - 1 - i] = value + depth if field == 0 else value
        set_masks(wet, NEAR - 1 - i, jnp.broadcast_to(wet_row(near, NEAR, i), (8, width)))
    for i in range(rows):
        sent, at, count = (to_near, i, NEAR) if i < NEAR else (to_far, i - rows + HALO, HALO)
        for field in range(3):
            value = sent[field * count + at]
            y[field, NEAR + i] = value + depth if field == 0 else value
        set_masks(wet, NEAR + i, jnp.broadcast_to(wet_row(sent, count, at), (8, width)))

    def keep(state, t):
        for field in range(3):
            strips[t, field] = state[field, pl.ds(NEAR + rows - 3 - t, 3)]

    keep(y, 0)

    for i in range(coarse_rows + 2):
        at = NEAR - 4 + 2 * i
        both = wet[0, at] * wet[0, at + 1]
        blocks = blocks_of(jnp.where(both > 0.0, 1.0, 0.0))
        coarse_wet[i] = jnp.concatenate([p * q for p, q in zip(blocks[0::2], blocks[1::2])], axis=1)
        for field in range(3):
            first[field, i] = restrict_pair(y[field, at], y[field, at + 1])

    def emit(i, values):
        for field in range(3):
            outcome[field, i - 1] = values[field]

    coarse_update(
        first, hv.at[:, :, pl.ds(0, half)], press.at[:, :, pl.ds(0, half)], lambda i: coarse_wet[i],
        coarse_rows + 2, range(1, coarse_rows + 1), kron_parts,
        lambda i: place.coarse_first + place.coarse_step * (i - 2), emit, place.near_inside,
    )
    order = matrix[...]
    arrived = ((3 * NEAR + 2, 0), (3 * NEAR + 2, half), (3 * NEAR + 3, 0))
    for field in range(3):
        old = [
            load_row(coarse_old, field, coarse_rows, half, place.own_row(coarse_rows, i))
            for i in range(coarse_rows)
        ]
        old = select(jnp.concatenate(old, axis=0), order, 2).reshape(coarse_rows, 8, half)
        plane, at = arrived[field]
        edge = turned(near[plane, :, at : at + half], field)
        if field == 0:
            old, edge = old + depth[:, :half], edge + depth[:, :half]
        coarse_before[field, 0] = edge
        coarse_before[field, 1:] = old * place.sign if field == 2 else old

    def coriolis_of(r):
        return place.first + place.step * (r - NEAR).astype(f32)

    def inside_of(r):
        return jnp.where(r < NEAR, place.near_inside, 1.0)

    def step(k, unused):
        for which, (source, target) in enumerate(((y, a), (a, b), (b, y))):
            s = 3 * k + which + 1
            run_stage(
                source, target, y, hv, press, wet, s, NEAR + rows - s, NEAR + rows - 2 * s, which, kron_parts,
                coriolis_of, inside_of,
            )

            @pl.when(s < HALO)
            def _():
                keep(target, s)

        return unused

    lax.fori_loop(0, STEPS, step, 0)
    for field in range(3):
        early_rows[field] = y[field, NEAR - 2 : NEAR + rows - HALO]


def far_kernel(
    rows, far, to_far, strips, early_rows, first, outcome, coarse_before, coarse_wet, short_parts, long_parts,
    depths,
    late_rows, delta, last_outcome, passed,
    y, a, b, hv, press, wet, state,
):
    width = y.shape[-1]
    origin = rows - HALO - 1
    own = rows - origin
    coarse_rows = rows // 2
    place = Place(rows)
    depth = depths[...]
    kron_parts = {GROUP: short_parts, CHUNK: long_parts}
    for field in range(3):
        for i in range(HALO):
            value = turned(far[(field + 1) * HALO - 1 - i], field)
            y[field, own + i] = value + depth if field == 0 else value
        state[field, : coarse_rows - 1] = first[field, 3:]
    for i in range(HALO):
        set_masks(wet, own + i, jnp.broadcast_to(wet_row(far, HALO, HALO - 1 - i), (8, width)))
        set_masks(wet, own - HALO + i, jnp.broadcast_to(wet_row(to_far, HALO, i), (8, width)))

    for field in range(3):
        state[field, coarse_rows - 1] = restrict_pair(y[field, own], y[field, own + 1])

    def emit(i, values):
        for field in range(3):
            last_outcome[field] = values[field]

    half = width // 2
    coarse_update(
        state, hv.at[:, :, pl.ds(0, half)], press.at[:, :, pl.ds(0, half)], lambda i: coarse_wet[coarse_rows + 1],
        coarse_rows, [coarse_rows - 2], kron_parts,
        lambda i: place.coarse_first + place.coarse_step * (coarse_rows - 1), emit,
    )

    def coriolis_of(r):
        return place.first + place.step * (r + origin).astype(f32)

    def inside_of(r):
        return jnp.where(r < own, 1.0, place.far_inside)

    def step(k, unused):
        for which, (source, target) in enumerate(((y, a), (a, b), (b, y))):
            t = 3 * k + which
            s = t + 1
            for field in range(3):
                for i in range(0 if which == 0 else 1, 3):
                    source[field, own - 3 - t + i] = strips[t, field, i]
            low = own - s
            run_stage(
                source, target, y, hv, press, wet, low, low + HALO, HALO, which, kron_parts, coriolis_of, inside_of
            )
        return unused

    lax.fori_loop(0, STEPS, step, 0)
    early = rows - HALO
    for field in range(3):
        late_rows[field] = y[field, own - HALO : own]
        for i in range(-1, coarse_rows):
            if 2 * i < early:
                pair = early_rows[field, 2 * i + 2], early_rows[field, 2 * i + 3]
            else:
                pair = y[field, 2 * i - origin], y[field, 2 * i + 1 - origin]
            difference = restrict_pair(*pair) - coarse_before[field, i + 1]
            delta[field, i + 1] = difference
            before = last_outcome[field] if i == coarse_rows - 1 else outcome[field, i + 1]
            passed[field, i + 1] = difference + before


def natural_kernel(rows, early_rows, late_rows, depths, matrix, natural):
    width = late_rows.shape[-1]
    place = Place(rows)
    depth = depths[...]
    for field in range(3):
        value = jnp.concatenate([part[field] for part in (early_rows.at[:, 2:], late_rows)], axis=0)
        if field == 0:
            value = value - depth
        if field == 2:
            value = value * place.sign
        for c, piece in select_blocks(value.reshape(rows * 8, width), matrix, 2):
            piece = piece.reshape(rows, 8, piece.shape[1])
            for r in range(rows):
                slices = tile_slices(rows, width, place.own_row(rows, r))
                for at in range(0, piece.shape[2], LANES):
                    natural[field, slices[(c + at) // LANES], :] = piece[r, :, at : at + LANES]


def final_kernel(
    rows, incoming, far_edge, previous, last_previous, coarse_wet, coarse_before, depths, long_parts, natural, order,
    spread,
    new_ends, coarse_new,
    state, hv, press, result, ends, coarse, semaphores,
):
    coarse_rows = rows // 2
    half = incoming.shape[-1]
    width = 2 * half
    place = Place(rows)
    depth = depths[:, :half]
    for field in range(3):
        state[field, : coarse_rows + 1] = incoming[field]
        state[field, coarse_rows + 1] = turned(far_edge[field], field)
    state[0, coarse_rows + 1] += (1.0 - place.far_inside) * depth
    kron_parts = {CHUNK: long_parts}

    def emit(i, values):
        for field in range(3):
            before = last_previous[field] if i == coarse_rows else previous[field, i]
            result[field, i - 1] = jnp.where(place.last, values[field], before)

    coarse_update(
        state, hv, press, lambda i: coarse_wet[i + 1], coarse_rows + 2, range(1, coarse_rows + 1), kron_parts,
        lambda i: place.coarse_first + place.coarse_step * (i - 1), emit,
    )
    to_natural = order[...]
    fine_rows = layer_major(place, rows, coarse_rows)
    own_rows = layer_major(place, coarse_rows, coarse_rows)
    copies = []
    for field in range(3):
        value = result[field].reshape(coarse_rows * 8, half)
        change = value - coarse_before[field, 1:].reshape(coarse_rows * 8, half)
        if field == 0:
            value = (result[0] - depth).reshape(coarse_rows * 8, half)
        if field == 2:
            value, change = value * place.sign, change * place.sign
        value = select(reorder(own_rows, value), to_natural, 2)
        for k in range(coarse_rows):
            for c in range(half // LANES):
                tile = pl.ds((k * (half // LANES) + c) * 8, 8)
                coarse[field, tile, :] = value[8 * k : 8 * k + 8, c * LANES : (c + 1) * LANES]
        copies.append(pltpu.make_async_copy(coarse.at[field], coarse_new.at[field], semaphores.at[3 + field]))
        copies[-1].start()
        for c, fine in select_blocks(reorder(fine_rows, change), spread, 2):
            for k in range(8 * rows // 8):
                for at in range(0, fine.shape[1], LANES):
                    tile = pl.ds((k * (width // LANES) + (c + at) // LANES) * 8, 8)
                    ends[field, tile, :] = natural[field, tile, :] + fine[8 * k : 8 * k + 8, at : at + LANES]
        copies.append(pltpu.make_async_copy(ends.at[field], new_ends.at[field], semaphores.at[field]))
        copies[-1].start()
    for copy in copies:
        copy.wait()


def middle_turn(incoming, far_edge, coarse_wet, mean_depth, coupling, place):
    signs = jnp.asarray([1.0, 1.0, -1.0], f32)[:, None, None]
    after = (far_edge * signs).at[0].add((1.0 - place.far_inside) * mean_depth[:, None])
    state = jnp.concatenate([incoming, after[:, None]], axis=1)
    incoming = incoming[:, 1:]
    h, u, v = state
    e = h - mean_depth[None, :, None]
    rows, layers, half = incoming.shape[1:]
    blocks = half // LANES
    p = jnp.einsum("kl,rlc->rkc", coupling, e, precision=lax.Precision.HIGHEST)

    def dx_parts(q):
        q = q.reshape(q.shape[0], layers, blocks, LANES)
        east = jnp.concatenate([q[:, :, 1:], jnp.roll(q[:, :, :1], -1, -1)], axis=2)
        west = jnp.concatenate([jnp.roll(q[:, :, -1:], 1, -1), q[:, :, :-1]], axis=2)
        return east.reshape(-1, layers, half)[1:-1], west.reshape(-1, layers, half)[1:-1]

    def dx(q):
        east, west = dx_parts(q)
        return (east - west) / 4.0

    def dy(q):
        return (q[2:] - q[:-2]) / 4.0

    def lap(q):
        east, west = dx_parts(q)
        return (q[2:] + q[:-2] + east + west - 4.0 * q[1:-1]) / 4.0

    um, vm = u[1:-1], v[1:-1]
    f = (place.coarse_first + place.coarse_step * jnp.arange(rows, dtype=f32))[:, None, None] / 4.0
    de = -(dx(h * u) + dy(h * v))
    du = coarse_wet * (-(um * dx(u) + vm * dy(u)) + f * vm - dx(p) + viscosity * lap(u))
    dv = coarse_wet * (-(um * dx(v) + vm * dy(v)) - f * um - dy(p) + viscosity * lap(v))
    return incoming + STEPS * time_step * jnp.stack([de, du, dv])


def local(starts, coarse_old, mean_depth, coupling, wet_cells):
    layers, rows, width = starts.shape[2:]
    coarse_rows, half = rows // 2, width // 2
    assert layers == 8 and rows % 8 == 0 and NEAR <= rows <= 2 * HALO
    tm, tm_size = lax.axis_index("tm"), lax.axis_size("tm")
    lat_size = lax.axis_size("lat")
    starts = tiles_of(starts[0])
    coarse_old = tiles_of(coarse_old[0])
    vmem = pl.BlockSpec(memory_space=pltpu.VMEM)
    hbm = pl.BlockSpec(memory_space=pltpu.HBM)
    fine_order = interleave_matrix(width)
    coarse_order = interleave_matrix(half)

    def array(*shape):
        return jax.ShapeDtypeStruct(shape, f32)

    def buffer(*shape):
        return pltpu.VMEM(shape, f32)

    def call(kernel, outs, in_specs, scratch=(), out_specs=None):
        return pl.pallas_call(
            functools.partial(kernel, rows),
            out_shape=outs,
            in_specs=in_specs,
            out_specs=out_specs or [vmem] * len(outs),
            scratch_shapes=list(scratch),
            compiler_params=pltpu.CompilerParams(vmem_limit_bytes=16 * 2**20),
        )

    near_of = [i + 1 if i % 2 == 0 else i - 1 for i in range(lat_size)]
    far_of = [i - 1 if i % 2 == 0 else i + 1 for i in range(lat_size)]

    def neighbours(of):
        return [(i, j) for i, j in enumerate(of) if 0 <= j < lat_size]

    def in_hbm(*operands):
        return [pltpu.with_memory_space_constraint(x, pltpu.HBM) for x in operands]

    to_far, starts_kept, fine_matrix, wet = call(
        pack_far_kernel,
        [
            array(3 * HALO + 2, 8, width),
            array(*starts.shape),
            jax.ShapeDtypeStruct((width, width), bf16),
            array(rows, width),
        ],
        [hbm] * 2,
        [pltpu.VMEM((rows, width), jnp.int32), pltpu.SemaphoreType.DMA((4,))],
    )(*in_hbm(starts, wet_cells))
    operands = (coarse_old, coupling, mean_depth.reshape(1, layers), jnp.asarray(coarse_order, bf16))
    far = lax.ppermute(to_far, "lat", neighbours(far_of))
    to_near, coarse_old, coupling_kept, mean_depths, order = call(
        pack_near_kernel,
        [array(3 * NEAR + 4, 8, width)] + [jax.ShapeDtypeStruct(x.shape, x.dtype) for x in operands],
        [vmem] * 4 + [hbm] * 4,
        [pltpu.SemaphoreType.DMA((4,))],
    )(starts_kept, fine_matrix, wet, to_far, *in_hbm(*operands))
    near = lax.ppermute(to_near, "lat", neighbours(near_of))

    def stage_scratch(count):
        return [buffer(3, count, 8, width)] * 3 + [buffer(count, 8, width)] * 2 + [buffer(6, count, 8, width)]

    early_rows, strips, coarse_before, first, outcome, coarse_wet, *shared = call(
        near_kernel,
        [array(3, rows - HALO + 2, 8, width), array(HALO, 3, 3, 8, width)]
        + [array(3, coarse_rows + n, 8, half) for n in (1, 2, 0)]
        + [array(coarse_rows + 2, 8, half)]
        + [jax.ShapeDtypeStruct((n * 8, 3 * n * 8), bf16) for n in (GROUP, CHUNK)]
        + [array(8, width)],
        [vmem] * 7,
        stage_scratch(NEAR + rows),
    )(near, to_near, to_far, coarse_old, mean_depths, coupling_kept, order)

    late_rows, delta, last_outcome, passed = call(
        far_kernel,
        [array(3, HALO, 8, width), array(3, coarse_rows + 1, 8, half), array(3, 8, half)]
        + [array(3, coarse_rows + 1, 8, half)],
        [vmem] * 11,
        stage_scratch(2 * HALO + 1) + [buffer(3, coarse_rows, 8, half)],
    )(far, to_far, strips, early_rows, first, outcome, coarse_before, coarse_wet, *shared)

    both = ("tm", "lat")

    def hand_on(current):
        def moved(values, of):
            pairs = [
                (t * lat_size + i, (t + 1) * lat_size + j)
                for t in range(tm_size - 1)
                for i, j in enumerate(of)
                if 0 <= j < lat_size
            ]
            return lax.ppermute(values, both, pairs)

        main, far_edge = moved(current, range(lat_size)), moved(current[:, -1], far_of)
        if current.shape[1] > coarse_rows:
            return main, far_edge
        near_edge = moved(current[:, 0], near_of) * jnp.asarray([1.0, 1.0, -1.0], f32)[:, None, None]
        near_edge = near_edge.at[0].add((1.0 - Place(rows).near_inside) * mean_depth[:, None])
        return jnp.concatenate([near_edge[:, None], main], axis=1), far_edge

    previous, last_previous = outcome, last_outcome
    incoming = hand_on(passed)
    (natural,) = call(natural_kernel, [array(*starts.shape)], [vmem] * 4)(
        early_rows, late_rows, shared[2], jnp.asarray(fine_order.T, bf16)
    )
    for turn in range(1, tm_size - 1):
        result = middle_turn(*incoming, coarse_wet[2:], mean_depth, coupling, Place(rows))
        previous = jnp.where(tm == turn, jnp.concatenate([previous[:, :1], result[:, :-1]], axis=1), previous)
        last_previous = jnp.where(tm == turn, result[:, -1], last_previous)
        incoming = hand_on(delta[:, 1:] + result)

    new_ends, coarse_new = call(
        final_kernel,
        [array(*starts.shape), array(*coarse_old.shape)],
        [vmem] * 11,
        [buffer(3, coarse_rows + 2, 8, half)]
        + [buffer(coarse_rows + 2, 8, half)] * 2
        + [buffer(3, coarse_rows, 8, half), buffer(*starts.shape), buffer(*coarse_old.shape)]
        + [pltpu.SemaphoreType.DMA((6,))],
        [hbm, hbm],
    )(
        *incoming, previous, last_previous, coarse_wet, coarse_before, shared[2], shared[1], natural,
        jnp.asarray(coarse_order.T, bf16), jnp.asarray(prolong_matrix(width), bf16),
    )
    return (
        from_tiles(new_ends, layers, rows, width)[None],
        from_tiles(coarse_new, layers, coarse_rows, half)[None],
    )


def solution(mesh):
    in_specs = (
        P("tm", None, None, "lat", None),
        P("tm", None, None, "lat", None),
        P(),
        P(),
        P("lat", None),
    )
    out_specs = (P("tm", None, None, "lat", None), P("tm", None, None, "lat", None))
    return jax.shard_map(local, mesh=mesh, in_specs=in_specs, out_specs=out_specs, check_vma=False)
```

```python
import functools

import jax
import jax.numpy as jnp
import numpy as np
from jax import lax
from jax.experimental import pallas as pl
from jax.experimental.pallas import tpu as pltpu
from jax.sharding import PartitionSpec as P


STEPS = 4
HALO = 3 * STEPS
NEAR = HALO + 2
GROUP = 6
CHUNK = GROUP + 2
LANES = 128

time_step = 0.15
viscosity = 0.02
rotation = 0.3

STAGE_WEIGHTS = (1.0, 0.25, 2.0 / 3.0)
STAGE_MIX = (None, (0.75, 0.25), (1.0 / 3.0, 2.0 / 3.0))
f32, bf16 = jnp.float32, jnp.bfloat16


def interleave_matrix(width):
    blocks = width // LANES
    place = np.arange(width)
    columns = blocks * (place % LANES) + place // LANES
    return (np.arange(width)[:, None] == columns[None, :]).astype(np.float32)


def prolong_matrix(width):
    half = width // 2
    blocks = half // LANES
    place = np.arange(half)
    columns = blocks * (place % LANES) + place // LANES
    return (columns[:, None] == np.arange(width)[None, :] // 2).astype(np.float32)


def tiles_of(x):
    fields, layers, rows, width = x.shape
    x = x.reshape(fields, layers, rows // 8, 8, width // LANES, LANES).transpose(0, 1, 2, 4, 3, 5)
    return x.reshape(fields, layers * rows * width // LANES, LANES)


def from_tiles(x, layers, rows, width):
    fields = x.shape[0]
    x = x.reshape(fields, layers, rows // 8, width // LANES, 8, LANES).transpose(0, 1, 2, 4, 3, 5)
    return x.reshape(fields, layers, rows, width)


def tile_slices(rows, width, r):
    blocks = width // LANES
    if not isinstance(r, int):
        start = lax.div(r, 8) * (8 * blocks) + lax.rem(r, 8)
    else:
        start = (r // 8) * (8 * blocks) + r % 8
    return [pl.ds(start + 8 * c, 8, stride=rows * blocks) for c in range(blocks)]


def load_row(tiles, field, rows, width, r):
    return jnp.concatenate([tiles[field, part, :] for part in tile_slices(rows, width, r)], axis=1)


def blocks_of(x):
    return [x[:, c : c + LANES] for c in range(0, x.shape[1], LANES)]


def east_west(x):
    blocks = blocks_of(x)
    east = jnp.concatenate(blocks[1:] + [pltpu.roll(blocks[0], LANES - 1, 1)], axis=1)
    west = jnp.concatenate([pltpu.roll(blocks[-1], 1, 1)] + blocks[:-1], axis=1)
    return east, west


def restrict_pair(north, south):
    blocks = blocks_of(north + south)
    return 0.25 * jnp.concatenate([a + b for a, b in zip(blocks[0::2], blocks[1::2])], axis=1)


def split(x, parts):
    found = []
    for _ in range(parts - 1):
        found.append(x.astype(bf16))
        x = x - found[-1].astype(f32)
    return found + [x.astype(bf16)]


def dot(a, b):
    return lax.dot_general(a, b, (((1,), (0,)), ((), ())), preferred_element_type=f32)


def select(x, matrix, parts):
    return sum(dot(part, matrix) for part in split(x, parts))


def select_blocks(x, matrix, parts, block=2 * LANES):
    terms = split(x, parts)
    for c in range(0, matrix.shape[1], block):
        yield c, sum(dot(part, matrix[:, c : c + block]) for part in terms)


def layer_major(place, rows, source_rows):
    repeat = rows // source_rows
    shape = (8 * rows, 8 * source_rows)
    target = lax.broadcasted_iota(jnp.int32, shape, 0)
    source = lax.broadcasted_iota(jnp.int32, shape, 1)
    layer = lax.div(target, rows)
    row = lax.div(place.own_row(rows, target - rows * layer), repeat)
    return jnp.where(source == 8 * row + layer, 1.0, 0.0).astype(bf16)


def reorder(matrix, x, parts=2):
    return sum(dot(matrix, part) for part in split(x, parts))


def coupling_parts(coupling, count):
    size = 8 * count
    high, low = split(jnp.concatenate([coupling] * count, axis=0), 2)
    layer = lax.broadcasted_iota(jnp.int32, (8, 3 * size), 0)
    column = lax.broadcasted_iota(jnp.int32, (8, 3 * size), 1)
    spread = jnp.where((column & 7) == layer, 1.0, 0.0).astype(bf16)
    row = lax.broadcasted_iota(jnp.int32, (size, 3 * size), 0)
    column = lax.broadcasted_iota(jnp.int32, (size, 3 * size), 1)
    third = jnp.where(column >= 2 * size, 2, jnp.where(column >= size, 1, 0))
    parts = jnp.where(third == 2, dot(low, spread), dot(high, spread))
    return jnp.where(((column - size * third) >> 3) == (row >> 3), parts, 0.0).astype(bf16)


def depth_of(mean_depth, width):
    row = lax.broadcasted_iota(jnp.int32, (8, 8), 0)
    column = lax.broadcasted_iota(jnp.int32, (8, 8), 1)
    diagonal = jnp.where(row == column, jnp.broadcast_to(mean_depth[...], (8, 8)), 0.0)
    return select(diagonal, jnp.ones((8, width), bf16), 3)


class Place:
    def __init__(self, rows):
        lat, lat_size = lax.axis_index("lat"), lax.axis_size("lat")
        tm, tm_size = lax.axis_index("tm"), lax.axis_size("tm")
        total = rows * lat_size
        self.even = lax.rem(lat, 2) == 0
        self.last = tm == tm_size - 1
        self.sign = jnp.where(self.even, -1.0, 1.0).astype(f32)
        low, high = (lat > 0).astype(f32), (lat < lat_size - 1).astype(f32)
        self.near_inside = jnp.where(self.even, high, low)
        self.far_inside = jnp.where(self.even, low, high)
        lat_f = lat.astype(f32)
        self.step = 4.0 * rotation / total
        self.coarse_step = 16.0 * rotation / total
        first = self.step * (lat_f * rows + 0.5) - 2.0 * rotation
        coarse = self.coarse_step * (lat_f * (rows // 2) + 0.5) - 4.0 * rotation
        self.first = jnp.where(self.even, -(first + self.step * (rows - 1)), first)
        self.coarse_first = jnp.where(self.even, -(coarse + self.coarse_step * (rows // 2 - 1)), coarse)

    def own_row(self, rows, i):
        return jnp.where(self.even, rows - 1 - i, i)


def pressure_rows(source, hv, press, start, count, kron_parts):
    h = source[0, pl.ds(start, count)]
    hv[pl.ds(start, count)] = h * source[2, pl.ds(start, count)]
    layers, width = h.shape[1:]
    high, low = split(h.reshape(count * layers, width), 2)
    p = dot(kron_parts[count][...], jnp.concatenate([high, low, high], axis=0))
    press[pl.ds(start, count)] = p.reshape(count, layers, width)


def row_tendency(source, hv, press, r, twice_viscosity, coriolis):
    h, u, v = source[0, r], source[1, r], source[2, r]
    u_north, u_south = source[1, r + 1], source[1, r - 1]
    v_north, v_south = source[2, r + 1], source[2, r - 1]
    hu_east, hu_west = east_west(h * u)
    divergence = (hu_east - hu_west) + (hv[r + 1] - hv[r - 1])
    u_east, u_west = east_west(u)
    v_east, v_west = east_west(v)
    p_east, p_west = east_west(press[r])
    to_east, to_west = twice_viscosity - u, twice_viscosity + u
    to_north, to_south = twice_viscosity - v, twice_viscosity + v
    zonal = (to_east * u_east + to_west * u_west) + (to_north * u_north + to_south * u_south)
    zonal = (zonal - (p_east - p_west)) + coriolis * v
    merid = (to_east * v_east + to_west * v_west) + (to_north * v_north + to_south * v_south)
    merid = (merid - (press[r + 1] - press[r - 1])) - coriolis * u
    return (h, u, v), (divergence, zonal, merid)


def run_stage(
    source, target, base, hv, press, wet, low, high, count, which, kron_parts, coriolis_of, inside_of
):
    factor = STAGE_WEIGHTS[which] * time_step / 2.0
    mix = STAGE_MIX[which]

    def one(r):
        here, rates = row_tendency(source, hv, press, r, 2.0 * viscosity, coriolis_of(r))
        mask, keep = wet[which, r], wet[3 + which, r]
        values = [here[0] if mix is None else mix[1] * here[0], keep * here[1], keep * here[2]]
        scales = (-factor * inside_of(r), mask, mask)
        for field in range(3):
            value = values[field]
            if mix is not None:
                value = value + mix[0] * base[field, r]
            target[field, r] = value + scales[field] * rates[field]

    def group(first):
        for i in range(GROUP):
            one(first + i)

    def fill(start, count):
        pressure_rows(source, hv, press, start, count, kron_parts)

    if isinstance(count, int):
        fill(low - 1, GROUP + 2)
        for first in range(0, count, GROUP):
            if first + GROUP < count:
                fill(low + first + GROUP + 1, GROUP)
            group(low + first)
        return

    def turn(k, unused):
        first = low + GROUP * k
        group(first)
        fill(jnp.minimum(first + GROUP + 1, high + 1 - GROUP), GROUP)
        return unused

    def two(k, unused):
        first = high - 2 * (rest - k)
        one(first)
        one(first + 1)
        return unused

    turns = lax.div(count, GROUP)
    rest = lax.div(count - GROUP * turns, 2)
    fill(jnp.minimum(low - 1, high - 1 - GROUP), GROUP + 2)
    lax.fori_loop(0, turns, turn, 0)
    lax.fori_loop(0, rest, two, 0)


def coarse_update(state, hv, press, wet_of, size, rows, kron_parts, coriolis_of, emit, inside=1.0):
    scale = STEPS * time_step / 4.0
    start = 0
    while start < size:
        pressure_rows(state, hv, press, min(start, size - CHUNK), CHUNK, kron_parts)
        start += CHUNK
    for i in rows:
        (h, u, v), (dh, du, dv) = row_tendency(state, hv, press, i, viscosity, coriolis_of(i))
        mask = wet_of(i) * scale
        keep = 1.0 - 4.0 * viscosity * mask
        step = scale * inside if i == rows[0] else scale
        emit(i, (h - step * dh, keep * u + mask * du, keep * v + mask * dv))


def wet_row(halo, count, i):
    plane, row = (0, i) if i < 8 else (1, i - count + 8)
    return halo[3 * count + plane, pl.ds(row, 1), :]


def set_masks(wet, i, mask):
    for which, weight in enumerate(STAGE_WEIGHTS):
        scaled = mask * (weight * time_step / 2.0)
        wet[which, i] = scaled
        wet[3 + which, i] = weight - 8.0 * viscosity * scaled


def turned(x, field):
    return -x if field == 2 else x


def order_of(width):
    blocks = width // LANES
    column = lax.broadcasted_iota(jnp.int32, (width, LANES), 0)
    column = column - blocks * lax.broadcasted_iota(jnp.int32, (width, LANES), 1)
    return jnp.concatenate([jnp.where(column == c, 1.0, 0.0).astype(bf16) for c in range(blocks)], axis=1)


def packed_rows(place, starts, order, rows, width, chosen):
    state = [
        load_row(starts, field, rows, width, place.own_row(rows, i)) * (place.sign if field == 2 else 1.0)
        for field in range(3)
        for i in chosen
    ]
    count = 8 * len(state)
    terms = jnp.concatenate(split(jnp.concatenate(state, axis=0), 2), axis=0)
    for c in range(0, width, 2 * LANES):
        value = dot(terms, order[:, c : c + 2 * LANES])
        yield c, (value[:count] + value[count:]).reshape(3, len(chosen), 8, 2 * LANES)


def pack_wet(place, packed, wet, rows, first, count):
    for plane, skip in ((0, 0), (1, count - 8)):
        for i in range(8):
            row = place.own_row(rows, first + skip + i)
            packed[3 * count + plane, pl.ds(i, 1), :] = wet[pl.ds(row, 1), :]


def pack_far_kernel(rows, starts_hbm, wet_hbm, to_far, starts, order, wet, wet_cells, semaphores):
    width = wet_cells.shape[-1]
    pairs = [(starts_hbm.at[field], starts.at[field]) for field in range(3)] + [(wet_hbm, wet_cells)]
    copies = [pltpu.make_async_copy(source, target, semaphores.at[n]) for n, (source, target) in enumerate(pairs)]
    for copy in copies:
        copy.start()
    place = Place(rows)
    order[...] = order_of(width)
    for copy in copies:
        copy.wait()
    for c, value in packed_rows(place, starts, order, rows, width, range(rows - HALO, rows)):
        for field in range(3):
            to_far[field * HALO : (field + 1) * HALO, :, c : c + value.shape[3]] = value[field]
    wet[...] = dot(wet_cells[...].astype(f32).astype(bf16), order[...])
    pack_wet(place, to_far, wet, rows, rows - HALO, HALO)


def pack_near_kernel(
    rows, starts, order, wet, to_far, coarse_hbm, coupling_hbm, depth_hbm, order_hbm,
    to_near, coarse_old, coupling, mean_depth, coarse_order,
    semaphores,
):
    width = wet.shape[-1]
    pairs = [(coarse_hbm, coarse_old), (coupling_hbm, coupling), (depth_hbm, mean_depth), (order_hbm, coarse_order)]
    copies = [pltpu.make_async_copy(source, target, semaphores.at[n]) for n, (source, target) in enumerate(pairs)]
    for copy in copies:
        copy.start()
    place = Place(rows)
    early = rows - HALO
    for c, value in packed_rows(place, starts, order, rows, width, range(early)):
        for field in range(3):
            to_near[field * NEAR : field * NEAR + early, :, c : c + value.shape[3]] = value[field]
    for field in range(3):
        to_near[field * NEAR + early : (field + 1) * NEAR] = to_far[field * HALO : field * HALO + NEAR - early]
    pack_wet(place, to_near, wet, rows, 0, NEAR)
    for copy in copies:
        copy.wait()
    half = width // 2
    old = [load_row(coarse_old, field, rows // 2, half, place.own_row(rows // 2, 0)) for field in range(3)]
    old[2] = old[2] * place.sign
    old = select(jnp.concatenate(old, axis=0), coarse_order[...], 2)
    to_near[3 * NEAR + 2, :, :half] = old[:8]
    to_near[3 * NEAR + 2, :, half:] = old[8:16]
    to_near[3 * NEAR + 3, :, :half] = old[16:]
    to_near[3 * NEAR + 3, :, half:] = old[16:]


def near_kernel(
    rows, near, to_near, to_far, coarse_old, mean_depth, coupling, matrix,
    early_rows, strips, coarse_before, first, outcome, coarse_wet, short_parts, long_parts, depths, wet,
    y, a, b, hv, press,
):
    width = y.shape[-1]
    half = width // 2
    coarse_rows = rows // 2
    place = Place(rows)
    depth = depth_of(mean_depth, width)
    depths[...] = depth
    kron_parts = {}
    for count, parts in ((GROUP, short_parts), (CHUNK, long_parts)):
        parts[...] = coupling_parts(coupling[...], count)
        kron_parts[count] = parts
    for i in range(NEAR):
        for field in range(3):
            value = turned(near[field * NEAR + i], field)
            y[field, NEAR - 1 - i] = value + depth if field == 0 else value
        set_masks(wet, NEAR - 1 - i, jnp.broadcast_to(wet_row(near, NEAR, i), (8, width)))
    for i in range(rows):
        sent, at, count = (to_near, i, NEAR) if i < NEAR else (to_far, i - rows + HALO, HALO)
        for field in range(3):
            value = sent[field * count + at]
            y[field, NEAR + i] = value + depth if field == 0 else value
        set_masks(wet, NEAR + i, jnp.broadcast_to(wet_row(sent, count, at), (8, width)))

    def keep(state, t):
        for field in range(3):
            strips[t, field] = state[field, pl.ds(NEAR + rows - 3 - t, 3)]

    keep(y, 0)

    for i in range(coarse_rows + 2):
        at = NEAR - 4 + 2 * i
        both = wet[0, at] * wet[0, at + 1]
        blocks = blocks_of(jnp.where(both > 0.0, 1.0, 0.0))
        coarse_wet[i] = jnp.concatenate([p * q for p, q in zip(blocks[0::2], blocks[1::2])], axis=1)
        for field in range(3):
            first[field, i] = restrict_pair(y[field, at], y[field, at + 1])

    def emit(i, values):
        for field in range(3):
            outcome[field, i - 1] = values[field]

    coarse_update(
        first, hv.at[:, :, pl.ds(0, half)], press.at[:, :, pl.ds(0, half)], lambda i: coarse_wet[i],
        coarse_rows + 2, range(1, coarse_rows + 1), kron_parts,
        lambda i: place.coarse_first + place.coarse_step * (i - 2), emit, place.near_inside,
    )
    order = matrix[...]
    arrived = ((3 * NEAR + 2, 0), (3 * NEAR + 2, half), (3 * NEAR + 3, 0))
    for field in range(3):
        old = [
            load_row(coarse_old, field, coarse_rows, half, place.own_row(coarse_rows, i))
            for i in range(coarse_rows)
        ]
        old = select(jnp.concatenate(old, axis=0), order, 2).reshape(coarse_rows, 8, half)
        plane, at = arrived[field]
        edge = turned(near[plane, :, at : at + half], field)
        if field == 0:
            old, edge = old + depth[:, :half], edge + depth[:, :half]
        coarse_before[field, 0] = edge
        coarse_before[field, 1:] = old * place.sign if field == 2 else old

    def coriolis_of(r):
        return place.first + place.step * (r - NEAR).astype(f32)

    def inside_of(r):
        return jnp.where(r < NEAR, place.near_inside, 1.0)

    def step(k, unused):
        for which, (source, target) in enumerate(((y, a), (a, b), (b, y))):
            s = 3 * k + which + 1
            run_stage(
                source, target, y, hv, press, wet, s, NEAR + rows - s, NEAR + rows - 2 * s, which, kron_parts,
                coriolis_of, inside_of,
            )

            @pl.when(s < HALO)
            def _():
                keep(target, s)

        return unused

    lax.fori_loop(0, STEPS, step, 0)
    for field in range(3):
        early_rows[field] = y[field, NEAR - 2 : NEAR + rows - HALO]


def far_kernel(
    rows, far, to_far, strips, early_rows, first, outcome, coarse_before, coarse_wet, short_parts, long_parts,
    depths, near_wet,
    late_rows, delta, last_outcome, passed, all_wet,
    y, a, b, hv, press, state,
):
    width = y.shape[-1]
    origin = rows - HALO - 1
    own = rows - origin
    wet = all_wet.at[:, pl.ds(NEAR + origin, 2 * HALO + 1)]
    coarse_rows = rows // 2
    place = Place(rows)
    depth = depths[...]
    kron_parts = {GROUP: short_parts, CHUNK: long_parts}
    for field in range(3):
        for i in range(HALO):
            value = turned(far[(field + 1) * HALO - 1 - i], field)
            y[field, own + i] = value + depth if field == 0 else value
        state[field, : coarse_rows - 1] = first[field, 3:]
    for i in range(HALO):
        set_masks(wet, own + i, jnp.broadcast_to(wet_row(far, HALO, HALO - 1 - i), (8, width)))

    for field in range(3):
        state[field, coarse_rows - 1] = restrict_pair(y[field, own], y[field, own + 1])

    def emit(i, values):
        for field in range(3):
            last_outcome[field] = values[field]

    half = width // 2
    coarse_update(
        state, hv.at[:, :, pl.ds(0, half)], press.at[:, :, pl.ds(0, half)], lambda i: coarse_wet[coarse_rows + 1],
        coarse_rows, [coarse_rows - 2], kron_parts,
        lambda i: place.coarse_first + place.coarse_step * (coarse_rows - 1), emit,
    )

    def coriolis_of(r):
        return place.first + place.step * (r + origin).astype(f32)

    def inside_of(r):
        return jnp.where(r < own, 1.0, place.far_inside)

    def step(k, unused):
        for which, (source, target) in enumerate(((y, a), (a, b), (b, y))):
            t = 3 * k + which
            s = t + 1
            for field in range(3):
                for i in range(0 if which == 0 else 1, 3):
                    source[field, own - 3 - t + i] = strips[t, field, i]
            low = own - s
            run_stage(
                source, target, y, hv, press, wet, low, low + HALO, HALO, which, kron_parts, coriolis_of, inside_of
            )
        return unused

    lax.fori_loop(0, STEPS, step, 0)
    early = rows - HALO
    for field in range(3):
        late_rows[field] = y[field, own - HALO : own]
        for i in range(-1, coarse_rows):
            if 2 * i < early:
                pair = early_rows[field, 2 * i + 2], early_rows[field, 2 * i + 3]
            else:
                pair = y[field, 2 * i - origin], y[field, 2 * i + 1 - origin]
            difference = restrict_pair(*pair) - coarse_before[field, i + 1]
            delta[field, i + 1] = difference
            before = last_outcome[field] if i == coarse_rows - 1 else outcome[field, i + 1]
            passed[field, i + 1] = difference + before


def natural_kernel(rows, early_rows, late_rows, depths, matrix, natural):
    width = late_rows.shape[-1]
    place = Place(rows)
    depth = depths[...]
    for field in range(3):
        value = jnp.concatenate([part[field] for part in (early_rows.at[:, 2:], late_rows)], axis=0)
        if field == 0:
            value = value - depth
        if field == 2:
            value = value * place.sign
        for c, piece in select_blocks(value.reshape(rows * 8, width), matrix, 2):
            piece = piece.reshape(rows, 8, piece.shape[1])
            for r in range(rows):
                slices = tile_slices(rows, width, place.own_row(rows, r))
                for at in range(0, piece.shape[2], LANES):
                    natural[field, slices[(c + at) // LANES], :] = piece[r, :, at : at + LANES]


def final_kernel(
    rows, incoming, far_edge, previous, last_previous, coarse_wet, coarse_before, depths, long_parts, natural, order,
    spread,
    new_ends, coarse_new,
    state, hv, press, result, ends, coarse, semaphores,
):
    coarse_rows = rows // 2
    half = incoming.shape[-1]
    width = 2 * half
    place = Place(rows)
    depth = depths[:, :half]
    for field in range(3):
        state[field, : coarse_rows + 1] = incoming[field]
        state[field, coarse_rows + 1] = turned(far_edge[field], field)
    state[0, coarse_rows + 1] += (1.0 - place.far_inside) * depth
    kron_parts = {CHUNK: long_parts}

    def emit(i, values):
        for field in range(3):
            before = last_previous[field] if i == coarse_rows else previous[field, i]
            result[field, i - 1] = jnp.where(place.last, values[field], before)

    coarse_update(
        state, hv, press, lambda i: coarse_wet[i + 1], coarse_rows + 2, range(1, coarse_rows + 1), kron_parts,
        lambda i: place.coarse_first + place.coarse_step * (i - 1), emit,
    )
    to_natural = order[...]
    fine_rows = layer_major(place, rows, coarse_rows)
    own_rows = layer_major(place, coarse_rows, coarse_rows)
    copies = []
    for field in range(3):
        value = result[field].reshape(coarse_rows * 8, half)
        change = value - coarse_before[field, 1:].reshape(coarse_rows * 8, half)
        if field == 0:
            value = (result[0] - depth).reshape(coarse_rows * 8, half)
        if field == 2:
            value, change = value * place.sign, change * place.sign
        value = select(reorder(own_rows, value), to_natural, 2)
        for k in range(coarse_rows):
            for c in range(half // LANES):
                tile = pl.ds((k * (half // LANES) + c) * 8, 8)
                coarse[field, tile, :] = value[8 * k : 8 * k + 8, c * LANES : (c + 1) * LANES]
        copies.append(pltpu.make_async_copy(coarse.at[field], coarse_new.at[field], semaphores.at[3 + field]))
        copies[-1].start()
        for c, fine in select_blocks(reorder(fine_rows, change), spread, 2):
            for k in range(8 * rows // 8):
                for at in range(0, fine.shape[1], LANES):
                    tile = pl.ds((k * (width // LANES) + (c + at) // LANES) * 8, 8)
                    ends[field, tile, :] = natural[field, tile, :] + fine[8 * k : 8 * k + 8, at : at + LANES]
        copies.append(pltpu.make_async_copy(ends.at[field], new_ends.at[field], semaphores.at[field]))
        copies[-1].start()
    for copy in copies:
        copy.wait()


def middle_turn(incoming, far_edge, coarse_wet, mean_depth, coupling, place):
    signs = jnp.asarray([1.0, 1.0, -1.0], f32)[:, None, None]
    after = (far_edge * signs).at[0].add((1.0 - place.far_inside) * mean_depth[:, None])
    state = jnp.concatenate([incoming, after[:, None]], axis=1)
    incoming = incoming[:, 1:]
    h, u, v = state
    e = h - mean_depth[None, :, None]
    rows, layers, half = incoming.shape[1:]
    blocks = half // LANES
    p = jnp.einsum("kl,rlc->rkc", coupling, e, precision=lax.Precision.HIGHEST)

    def dx_parts(q):
        q = q.reshape(q.shape[0], layers, blocks, LANES)
        east = jnp.concatenate([q[:, :, 1:], jnp.roll(q[:, :, :1], -1, -1)], axis=2)
        west = jnp.concatenate([jnp.roll(q[:, :, -1:], 1, -1), q[:, :, :-1]], axis=2)
        return east.reshape(-1, layers, half)[1:-1], west.reshape(-1, layers, half)[1:-1]

    def dx(q):
        east, west = dx_parts(q)
        return (east - west) / 4.0

    def dy(q):
        return (q[2:] - q[:-2]) / 4.0

    def lap(q):
        east, west = dx_parts(q)
        return (q[2:] + q[:-2] + east + west - 4.0 * q[1:-1]) / 4.0

    um, vm = u[1:-1], v[1:-1]
    f = (place.coarse_first + place.coarse_step * jnp.arange(rows, dtype=f32))[:, None, None] / 4.0
    de = -(dx(h * u) + dy(h * v))
    du = coarse_wet * (-(um * dx(u) + vm * dy(u)) + f * vm - dx(p) + viscosity * lap(u))
    dv = coarse_wet * (-(um * dx(v) + vm * dy(v)) - f * um - dy(p) + viscosity * lap(v))
    return incoming + STEPS * time_step * jnp.stack([de, du, dv])


def local(starts, coarse_old, mean_depth, coupling, wet_cells):
    layers, rows, width = starts.shape[2:]
    coarse_rows, half = rows // 2, width // 2
    assert layers == 8 and rows % 8 == 0 and NEAR <= rows <= 2 * HALO
    tm, tm_size = lax.axis_index("tm"), lax.axis_size("tm")
    lat_size = lax.axis_size("lat")
    starts = tiles_of(starts[0])
    coarse_old = tiles_of(coarse_old[0])
    vmem = pl.BlockSpec(memory_space=pltpu.VMEM)
    hbm = pl.BlockSpec(memory_space=pltpu.HBM)
    fine_order = interleave_matrix(width)
    coarse_order = interleave_matrix(half)

    def array(*shape):
        return jax.ShapeDtypeStruct(shape, f32)

    def buffer(*shape):
        return pltpu.VMEM(shape, f32)

    def call(kernel, outs, in_specs, scratch=(), out_specs=None, aliases=None):
        return pl.pallas_call(
            functools.partial(kernel, rows),
            out_shape=outs,
            in_specs=in_specs,
            out_specs=out_specs or [vmem] * len(outs),
            scratch_shapes=list(scratch),
            input_output_aliases=aliases or {},
            compiler_params=pltpu.CompilerParams(vmem_limit_bytes=16 * 2**20),
        )

    near_of = [i + 1 if i % 2 == 0 else i - 1 for i in range(lat_size)]
    far_of = [i - 1 if i % 2 == 0 else i + 1 for i in range(lat_size)]

    def neighbours(of):
        return [(i, j) for i, j in enumerate(of) if 0 <= j < lat_size]

    def in_hbm(*operands):
        return [pltpu.with_memory_space_constraint(x, pltpu.HBM) for x in operands]

    to_far, starts_kept, fine_matrix, wet = call(
        pack_far_kernel,
        [
            array(3 * HALO + 2, 8, width),
            array(*starts.shape),
            jax.ShapeDtypeStruct((width, width), bf16),
            array(rows, width),
        ],
        [hbm] * 2,
        [pltpu.VMEM((rows, width), jnp.int32), pltpu.SemaphoreType.DMA((4,))],
    )(*in_hbm(starts, wet_cells))
    operands = (coarse_old, coupling, mean_depth.reshape(1, layers), jnp.asarray(coarse_order, bf16))
    far = lax.ppermute(to_far, "lat", neighbours(far_of))
    to_near, coarse_old, coupling_kept, mean_depths, order = call(
        pack_near_kernel,
        [array(3 * NEAR + 4, 8, width)] + [jax.ShapeDtypeStruct(x.shape, x.dtype) for x in operands],
        [vmem] * 4 + [hbm] * 4,
        [pltpu.SemaphoreType.DMA((4,))],
    )(starts_kept, fine_matrix, wet, to_far, *in_hbm(*operands))
    near = lax.ppermute(to_near, "lat", neighbours(near_of))

    def stage_scratch(count):
        return [buffer(3, count, 8, width)] * 3 + [buffer(count, 8, width)] * 2

    early_rows, strips, coarse_before, first, outcome, coarse_wet, *shared = call(
        near_kernel,
        [array(3, rows - HALO + 2, 8, width), array(HALO, 3, 3, 8, width)]
        + [array(3, coarse_rows + n, 8, half) for n in (1, 2, 0)]
        + [array(coarse_rows + 2, 8, half)]
        + [jax.ShapeDtypeStruct((n * 8, 3 * n * 8), bf16) for n in (GROUP, CHUNK)]
        + [array(8, width), array(6, NEAR + rows + HALO, 8, width)],
        [vmem] * 7,
        stage_scratch(NEAR + rows),
    )(near, to_near, to_far, coarse_old, mean_depths, coupling_kept, order)

    late_rows, delta, last_outcome, passed, _ = call(
        far_kernel,
        [array(3, HALO, 8, width), array(3, coarse_rows + 1, 8, half), array(3, 8, half)]
        + [array(3, coarse_rows + 1, 8, half), array(6, NEAR + rows + HALO, 8, width)],
        [vmem] * 12,
        stage_scratch(2 * HALO + 1) + [buffer(3, coarse_rows, 8, half)],
        aliases={11: 4},
    )(far, to_far, strips, early_rows, first, outcome, coarse_before, coarse_wet, *shared)

    both = ("tm", "lat")

    def hand_on(current):
        def moved(values, of):
            pairs = [
                (t * lat_size + i, (t + 1) * lat_size + j)
                for t in range(tm_size - 1)
                for i, j in enumerate(of)
                if 0 <= j < lat_size
            ]
            return lax.ppermute(values, both, pairs)

        main, far_edge = moved(current, range(lat_size)), moved(current[:, -1], far_of)
        if current.shape[1] > coarse_rows:
            return main, far_edge
        near_edge = moved(current[:, 0], near_of) * jnp.asarray([1.0, 1.0, -1.0], f32)[:, None, None]
        near_edge = near_edge.at[0].add((1.0 - Place(rows).near_inside) * mean_depth[:, None])
        return jnp.concatenate([near_edge[:, None], main], axis=1), far_edge

    previous, last_previous = outcome, last_outcome
    incoming = hand_on(passed)
    (natural,) = call(natural_kernel, [array(*starts.shape)], [vmem] * 4)(
        early_rows, late_rows, shared[2], jnp.asarray(fine_order.T, bf16)
    )
    for turn in range(1, tm_size - 1):
        result = middle_turn(*incoming, coarse_wet[2:], mean_depth, coupling, Place(rows))
        previous = jnp.where(tm == turn, jnp.concatenate([previous[:, :1], result[:, :-1]], axis=1), previous)
        last_previous = jnp.where(tm == turn, result[:, -1], last_previous)
        incoming = hand_on(delta[:, 1:] + result)

    new_ends, coarse_new = call(
        final_kernel,
        [array(*starts.shape), array(*coarse_old.shape)],
        [vmem] * 11,
        [buffer(3, coarse_rows + 2, 8, half)]
        + [buffer(coarse_rows + 2, 8, half)] * 2
        + [buffer(3, coarse_rows, 8, half), buffer(*starts.shape), buffer(*coarse_old.shape)]
        + [pltpu.SemaphoreType.DMA((6,))],
        [hbm, hbm],
    )(
        *incoming, previous, last_previous, coarse_wet, coarse_before, shared[2], shared[1], natural,
        jnp.asarray(coarse_order.T, bf16), jnp.asarray(prolong_matrix(width), bf16),
    )
    return (
        from_tiles(new_ends, layers, rows, width)[None],
        from_tiles(coarse_new, layers, coarse_rows, half)[None],
    )


def solution(mesh):
    in_specs = (
        P("tm", None, None, "lat", None),
        P("tm", None, None, "lat", None),
        P(),
        P(),
        P("lat", None),
    )
    out_specs = (P("tm", None, None, "lat", None), P("tm", None, None, "lat", None))
    return jax.shard_map(local, mesh=mesh, in_specs=in_specs, out_specs=out_specs, check_vma=False)
```
